32 devices in a mesh: row: 8 (over z, x), col: 4 (over y, core).
Axes of the slice: x: 2, y: 2, z: 4, core: 2. Of those that a mesh axis runs over, the one named last changes fastest.
Arguments:
- start_vec: float32 [4, 1024, 256], P(None, 'row'), may hold values from -6.2 to 6.2
- cond_orb: bfloat16 [1024, 16384], P('row', 'col'), may hold values from -6 to 6
- val_orb: bfloat16 [256, 16384], P('row', 'col'), may hold values from -6 to 6
- kernel: float32 [16384, 16384], P('row', 'col'), may hold values from -7.1525574e-07 to 7.1525574e-07
- cond_energy: float32 [1024], P('row'), may hold values from 1 to 3
- val_energy: float32 [256], replicated, may hold values from -2 to 0
Outputs:
- right_next: float32 [4, 1024, 256], P(None, 'row')
- left_next: float32 [4, 1024, 256], P(None, 'row')
- coefs: float32 [4, 4], replicated
The draws below stay inside these ranges and needn't reach their ends.
All inputs are finite; a program needn't handle non-finite values.
Results may differ from the reference program's by a relative error of at most 0.0046.
Values may be sent and summed in bfloat16 or wider, within the bound.
A program may use at most 128 MiB of HBM per device.

```python
import math
import jax
import jax.numpy as jnp
from jax import lax

NC = 1024
NV = 256
NP = 16384
NB = 4
ITERS = 2


def draw_energies(key):
    cond_key = jax.random.fold_in(key, 101)
    val_key = jax.random.fold_in(key, 202)
    cond_levels = jax.random.uniform(cond_key, (NC,), jnp.float32, 1.0, 3.0)
    val_levels = jax.random.uniform(val_key, (NV,), jnp.float32, -2.0, 0.0)
    return (cond_levels, val_levels)


def draw_cond_energy(key, part):
    return draw_energies(key)[0]


def draw_val_energy(key, part):
    return draw_energies(key)[1]


def draw_start_vec(key, part):
    cond_levels, val_levels = draw_energies(key)
    pair_energy = cond_levels[:, None] - val_levels[None, :]
    ranks = jax.random.permutation(jax.random.fold_in(key, 303), NB)
    narrow = ranks < NB // 2
    log_width = jax.random.uniform(jax.random.fold_in(key, 404), (NB,), jnp.float32, math.log(0.03), math.log(0.1))
    widths = jnp.exp(log_width)
    centers = jax.random.uniform(jax.random.fold_in(key, 505), (NB,), jnp.float32, 2.0, 4.0)
    offset = (pair_energy[None] - centers[:, None, None]) / widths[:, None, None]
    envelope = jnp.where(narrow[:, None, None], jnp.exp(-0.5 * offset * offset) + 0.03, 1.0)
    noise_key = jax.random.fold_in(key, 606)
    noise = jax.random.truncated_normal(noise_key, -6.0, 6.0, (NB, NC, NV), jnp.float32)
    return noise * envelope


def block_levels(key, shape, pieces, smallest, top_value):
    def one(dim, blocks):
        heights = jax.random.uniform(jax.random.fold_in(jax.random.fold_in(key, 6), dim), (blocks,), jnp.float32, smallest / len(pieces), top_value / len(pieces))
        return jnp.repeat(jnp.exp(heights), shape[dim] // blocks).reshape((-1,) + (1,) * (len(shape) - dim - 1))

    gain = one(*pieces[0])
    for cut in pieces[1:]:
        gain = gain * one(*cut)
    return gain


def bell_draw(rng, dims, scale, most, shards=(), kind=jnp.bfloat16):
    entries = scale * jax.random.normal(rng, dims, jnp.float32)
    if shards:
        entries = entries * block_levels(rng, dims, shards, -0.22, 0.18)
    return jnp.clip(entries, -most, most).astype(kind)


def setup_inputs(seed: int = 0) -> dict:
    splits = jax.random.split(jax.random.key(seed), 7)
    start_vec = draw_start_vec(jax.random.fold_in(splits[6], 71), 0)
    cond_orb = bell_draw(splits[1], (NC, NP), 1.0, 6.0, ((0, 8), (1, 4)))
    val_orb = bell_draw(splits[2], (NV, NP), 1.0, 6.0, ((0, 8), (1, 4)))
    kernel = bell_draw(splits[3], (NP, NP), (NP * NP * NC * NV) ** -0.5, 7.152557373046875e-07, ((0, 8), (1, 4)), jnp.float32)
    cond_energy = draw_cond_energy(jax.random.fold_in(splits[6], 71), 0)
    val_energy = draw_val_energy(jax.random.fold_in(splits[6], 71), 0)
    return dict(start_vec=start_vec, cond_orb=cond_orb, val_orb=val_orb, kernel=kernel, cond_energy=cond_energy, val_energy=val_energy)


def apply_both(stack, cond_orb, val_orb, kernel, energy):
    cond_f = cond_orb.astype(jnp.float32)

    def forward(vector):
        paired = jnp.dot(vector.astype(jnp.bfloat16), val_orb, preferred_element_type=jnp.float32)
        return lax.optimization_barrier(jnp.sum(paired * cond_f, axis=0))
    coeff = lax.map(forward, stack)
    half = coeff.shape[0] // 2
    right = jnp.dot(coeff[:half], kernel.T, precision=lax.Precision.HIGHEST, preferred_element_type=jnp.float32)
    left = jnp.dot(coeff[half:], kernel, precision=lax.Precision.HIGHEST, preferred_element_type=jnp.float32)
    zed = jnp.concatenate([right, left], axis=0)

    def backward(weights):
        weighted = (cond_f * weights[None, :]).astype(jnp.bfloat16)
        return lax.dot_general(weighted, val_orb, (((1,), (1,)), ((), ())), preferred_element_type=jnp.float32)
    return energy[None] * stack + lax.map(backward, zed)

def inner(first, second):
    return lax.optimization_barrier(jnp.sum(first * second, axis=(1, 2)))

def reference(start_vec, cond_orb, val_orb, kernel, cond_energy, val_energy):
    energy = cond_energy[:, None] - val_energy[None, :]
    count = start_vec.shape[0]
    norm_sq = inner(start_vec, start_vec)
    right = start_vec / jnp.sqrt(norm_sq)[:, None, None]
    left = right
    right_old = jnp.zeros_like(right)
    left_old = jnp.zeros_like(left)
    record = []
    for step in range(ITERS):
        images = apply_both(jnp.concatenate([right, left], axis=0), cond_orb, val_orb, kernel, energy)
        image_r = images[:count]
        image_l = images[count:]
        alpha = inner(left, image_r)
        mu_co = inner(left_old, image_r)
        nu_co = inner(right_old, image_l)
        resid_r = image_r - alpha[:, None, None] * right - mu_co[:, None, None] * right_old
        resid_l = image_l - alpha[:, None, None] * left - nu_co[:, None, None] * left_old
        cross = inner(resid_l, resid_r)
        bound = jnp.maximum(cross, 0.25 * jnp.sqrt(inner(resid_r, resid_r) * inner(resid_l, resid_l)))
        beta = jnp.sqrt(bound)
        right_old, left_old = (right, left)
        right = resid_r / beta[:, None, None]
        left = resid_l / beta[:, None, None]
        record.append(alpha)
        record.append(beta)
    return (right, left, jnp.stack(record, axis=1))
```

```python
import functools

import jax
import jax.numpy as jnp
from jax import lax
from jax.experimental import pallas as pl
from jax.experimental.pallas import tpu as pltpu
from jax.sharding import PartitionSpec as P

ITERS = 2


def inner_local(first, second):
    return jnp.sum(first * second, axis=(1, 2))


def shards(start_vec, cond_orb, val_orb, kernel, cond_energy, val_energy):
    count = start_vec.shape[0]
    row_place = lax.axis_index("row")
    col_place = lax.axis_index("col")
    span_row = kernel.shape[0]
    span_col = kernel.shape[1]
    panel = lax.all_gather(val_orb, "row", axis=0, tiled=True)
    cond_f = cond_orb.astype(jnp.float32)
    energy = cond_energy[:, None] - val_energy[None, :]

    def row_total(values):
        return lax.psum(values, "row")

    def col_total(values):
        return lax.psum(values, "col")

    def reduce_dots(terms):
        return row_total(terms)

    (norm_sq,) = reduce_dots((inner_local(start_vec, start_vec),))
    right = start_vec / jnp.sqrt(norm_sq)[:, None, None]
    left = right
    right_old = jnp.zeros_like(right)
    left_old = jnp.zeros_like(left)
    record = []
    for step in range(ITERS):
        stack = jnp.concatenate([right, left], axis=0)
        rounded = stack.astype(jnp.bfloat16)
        paired = jnp.einsum("bcv,vn->bcn", rounded, panel, preferred_element_type=jnp.float32)
        partial_value = jnp.sum(paired * cond_f[None], axis=1)
        folded = row_total(partial_value)
        right_coeff = folded[:count]
        left_coeff = folded[count:]
        left_all = lax.all_gather(left_coeff, "col", axis=1, tiled=True)
        left_rows = lax.dynamic_slice_in_dim(left_all, row_place * span_row, span_row, 1)
        right_part = jnp.einsum(
            "bn,mn->bm",
            right_coeff,
            kernel,
            precision=lax.Precision.HIGHEST,
            preferred_element_type=jnp.float32,
        )
        left_part = jnp.einsum(
            "bm,mn->bn",
            left_rows,
            kernel,
            precision=lax.Precision.HIGHEST,
            preferred_element_type=jnp.float32,
        )
        right_zed = col_total(right_part)
        left_zed = row_total(left_part)
        right_all = lax.all_gather(right_zed, "row", axis=1, tiled=True)
        right_cols = lax.dynamic_slice_in_dim(right_all, col_place * span_col, span_col, 1)
        zed = jnp.concatenate([right_cols, left_zed], axis=0)
        weighted = (cond_f[None] * zed[:, None, :]).astype(jnp.bfloat16)
        image_terms = jnp.einsum("bcn,vn->bcv", weighted, panel, preferred_element_type=jnp.float32)
        kernel_part = col_total(image_terms)
        images = energy[None] * stack + kernel_part
        image_r = images[:count]
        image_l = images[count:]
        table = reduce_dots(
            (
                inner_local(left, image_r),
                inner_local(left_old, image_r),
                inner_local(right_old, image_l),
                inner_local(image_l, image_r),
                inner_local(image_l, right),
                inner_local(left, right),
                inner_local(left, right_old),
                inner_local(left_old, right),
                inner_local(left_old, right_old),
                inner_local(image_r, image_r),
                inner_local(right, right),
                inner_local(right_old, right_old),
                inner_local(image_r, right),
                inner_local(image_r, right_old),
                inner_local(right, right_old),
                inner_local(image_l, image_l),
                inner_local(left, left),
                inner_local(left_old, left_old),
                inner_local(image_l, left),
                inner_local(image_l, left_old),
                inner_local(left, left_old),
            )
        )
        alpha, mu_co, nu_co = (table[0], table[1], table[2])
        cross = (
            table[3]
            - alpha * table[4]
            - mu_co * nu_co
            - alpha * alpha
            + alpha * alpha * table[5]
            + alpha * mu_co * table[6]
            - nu_co * mu_co
            + nu_co * alpha * table[7]
            + nu_co * mu_co * table[8]
        )
        right_sq = (
            table[9]
            + alpha * alpha * table[10]
            + mu_co * mu_co * table[11]
            - 2.0 * alpha * table[12]
            - 2.0 * mu_co * table[13]
            + 2.0 * alpha * mu_co * table[14]
        )
        left_sq = (
            table[15]
            + alpha * alpha * table[16]
            + nu_co * nu_co * table[17]
            - 2.0 * alpha * table[18]
            - 2.0 * nu_co * table[19]
            + 2.0 * alpha * nu_co * table[20]
        )
        resid_r = image_r - alpha[:, None, None] * right - mu_co[:, None, None] * right_old
        resid_l = image_l - alpha[:, None, None] * left - nu_co[:, None, None] * left_old
        bound = jnp.maximum(cross, 0.25 * jnp.sqrt(right_sq * left_sq))
        beta = jnp.sqrt(bound)
        right_old, left_old = (right, left)
        right = resid_r / beta[:, None, None]
        left = resid_l / beta[:, None, None]
        record.append(alpha)
        record.append(beta)
    joined = jnp.concatenate([right, left], axis=0)
    return (joined[:count], joined[count:], jnp.stack(record, axis=1))


MESH = pl.DeviceIdType.MESH
TERMS = 24
ROWS_K = 256


def fits(mesh, start_vec, cond_orb, val_orb, kernel, cond_energy, val_energy):
    R, C = mesh.shape["row"], mesh.shape["col"]
    points = kernel.shape[0]
    chunk = points // (R * C)
    local = cond_orb.shape[0] // R
    kernel_bytes = 2 * (points // R) * (points // C)
    return (
        start_vec.shape[0] == 4
        and R % 2 == 0
        and C == 4
        and chunk % ROWS_K == 0
        and local % 32 == 0
        and (val_orb.shape[0] // R) % 16 == 0
        and val_orb.shape[0] == 256
        and kernel_bytes <= 16 * 2**20
    )


def body_kernel(
    R, C,
    start, cond, val, kmat, energy,
    out_r, out_l, out_c,
    panel, kb, kf, xs, xb, img, wbuf, lhs_r, lhs_l, lacc, terms,
    a_send, a_recv, b_row, b_left, c_rsend, c_rrecv, c_lsend, c_lrecv, d_row,
    e_send, e_recv, y_all, g_all, t_all,
    k_sem, p_up, p_dn, p_x, p_recv,
    a_ss, a_rs, b_ss, b_rs, bl_ss, bl_rs, cr_ss, cr_rs, cl_ss, cl_rs, d_ss, d_rs,
    e_ss, e_rs, y_ss, y_rs, g_ss, g_rs, t_ss, t_rs,
):
    row = lax.axis_index("row")
    col = lax.axis_index("col")
    count = start.shape[0]
    stack = 2 * count
    nc = start.shape[1]
    nv = start.shape[2]
    half = nc // 2
    chunk = a_send.shape[-1]
    span_row = kb.shape[0]
    span_col = kb.shape[1]
    Y = C // 2
    core = lax.rem(col, 2)
    ypos = col // 2
    mate = ypos * 2 + 1 - core
    f32, bf16 = jnp.float32, jnp.bfloat16
    mine = col * R + row
    owner_row = mine // C
    slot_left = lax.rem(mine, C)

    def remote(src, dst, ss, rs, to_row, to_col):
        return pltpu.make_async_remote_copy(
            src_ref=src, dst_ref=dst, send_sem=ss, recv_sem=rs,
            device_id=(to_row, to_col), device_id_type=MESH,
        )

    def away(k):
        return lax.rem(row + k, R)

    barrier = pltpu.get_barrier_semaphore()

    @pl.loop(1, R * C)
    def _(k):
        flat = lax.rem(row * C + col + k, R * C)
        pl.semaphore_signal(barrier, inc=1, device_id=(flat // C, lax.rem(flat, C)), device_id_type=MESH)

    def kcopy(i, slot):
        return pltpu.make_async_copy(
            kmat.at[pl.ds(i * ROWS_K, ROWS_K), :], kf.at[slot], k_sem.at[slot]
        )

    kcopy(0, 0).start()
    kcopy(1, 1).start()
    panel[row] = val[...]

    for b in range(count):
        sq = jnp.sum(start[b] * start[b], axis=0, keepdims=True)
        terms[b, 0:1, :] = sq[:, :128] + sq[:, 128:]
    lane = lax.broadcasted_iota(jnp.int32, (8, 128), 1)
    tile = jnp.zeros((8, 128), f32)
    for b in range(count):
        total = jnp.sum(terms[b, 0:1, :], axis=1, keepdims=True)
        tile = tile + jnp.where(lane == b, total, 0.0)
    t_all[0, row, 0:8, :] = tile
    t_all[0, row, 8:TERMS, :] = jnp.zeros((TERMS - 8, 128), f32)

    pl.semaphore_wait(barrier, R * C - 1)

    def table_start(i):
        @pl.loop(1, R)
        def _(k):
            peer = away(k)
            remote(t_all.at[i, row], t_all.at[i, row], t_ss.at[i, peer], t_rs.at[i, row], peer, col).start()

    def table_wait(i):
        @pl.loop(1, R)
        def _(k):
            peer = away(k)
            remote(t_all.at[i, row], t_all.at[i, peer], t_ss.at[i, peer], t_rs.at[i, peer], peer, col).wait_recv()
        total = t_all[i, 0]
        for k in range(1, R):
            total = total + t_all[i, k]
        return total

    table_start(0)

    L = R // 2
    line = row // 2
    side = lax.rem(row, 2)
    pair = line * 2 + 1 - side

    def blk(block, sem, to_row):
        return remote(panel.at[block], panel.at[block], sem.at[block], p_recv.at[block], to_row, col)

    def pass_on(block, up, down):
        if up:
            @pl.when(line + 1 < L)
            def _():
                blk(block, p_up, row + 2).start()
        if down:
            @pl.when(line >= 1)
            def _():
                blk(block, p_dn, row - 2).start()
        blk(block, p_x, pair).start()

    pass_on(row, True, True)

    n_k = span_row // ROWS_K

    def take_k(i):
        slot = lax.rem(i, 2)
        kcopy(i, slot).wait()
        base = pl.multiple_of(i * ROWS_K, ROWS_K)

        @pl.loop(0, ROWS_K // 16)
        def _(g):
            at = pl.multiple_of(g * 16, 16)
            kb[pl.ds(pl.multiple_of(base + at, 16), 16), :] = kf[slot, pl.ds(at, 16), :].astype(bf16)

        @pl.when(i + 2 < n_k)
        def _():
            kcopy(i + 2, slot).start()

    per = n_k // L
    for d in range(L):
        @pl.loop(d * per, n_k if d == L - 1 else (d + 1) * per)
        def _(i):
            take_k(i)
        if d == 0:
            total = table_wait(0)
            scale = 1.0 / jnp.sqrt(total[0:1, :])
            for b in range(count):
                q = start[b] * scale[:, b:b + 1]
                xs[0, b] = q
                xs[0, count + b] = q
                xb[b] = q.astype(bf16)
        if d + 1 < L:
            @pl.when(line - (d + 1) >= 0)
            def _():
                block = row - 2 * (d + 1)
                blk(block, p_x, pair).wait_recv()
                pass_on(block, True, False)

            @pl.when(line + (d + 1) < L)
            def _():
                block = row + 2 * (d + 1)
                blk(block, p_x, pair).wait_recv()
                pass_on(block, False, True)

    @pl.loop(0, L)
    def _(z):
        blk(z * 2 + 1 - side, p_x, pair).wait_recv()

    for it in range(ITERS):
        wide = count if it == 0 else stack

        @pl.loop(1, R + 1)
        def _(k):
            peer = away(k)
            at = pl.multiple_of(peer * chunk, chunk)
            block = panel[:, :, pl.ds(at, chunk)].reshape(nv, chunk)
            weight = cond[:, pl.ds(at, chunk)].astype(f32)
            for b in range(wide):
                paired = jnp.dot(xb[b], block, preferred_element_type=f32)
                value = jnp.sum(paired * weight, axis=0, keepdims=True)
                a_send[it, peer, b:b + 1, :] = value
                if wide == count:
                    a_send[it, peer, count + b:count + b + 1, :] = value

            @pl.when(k < R)
            def _():
                remote(a_send.at[it, peer], a_recv.at[it, row], a_ss.at[it, peer], a_rs.at[it, row], peer, col).start()

        @pl.loop(1, R)
        def _(k):
            peer = away(k)
            remote(a_send.at[it, peer], a_recv.at[it, peer], a_ss.at[it, peer], a_rs.at[it, peer], peer, col).wait_recv()
        a_recv[it, row] = a_send[it, row]
        coeff = a_recv[it, 0]
        for k in range(1, R):
            coeff = coeff + a_recv[it, k]

        b_row[it, row] = coeff
        for j in range(C):
            here = jnp.logical_and(owner_row == row, col == j)

            @pl.when(here)
            def _():
                b_left[it, slot_left] = coeff

            @pl.when(jnp.logical_not(here))
            def _():
                remote(b_row.at[it, row], b_left.at[it, slot_left], bl_ss.at[it, j], bl_rs.at[it, slot_left], owner_row, j).start()

        @pl.loop(1, R)
        def _(k):
            peer = away(k)
            remote(b_row.at[it, row], b_row.at[it, row], b_ss.at[it, peer], b_rs.at[it, row], peer, col).start()

        def split(ref, dst, pieces):
            for j in range(pieces):
                piece = ref[it, j]
                high = piece.astype(bf16)
                low = (piece - high.astype(f32)).astype(bf16)
                dst[:, j * chunk:(j + 1) * chunk] = jnp.concatenate([high, low], axis=0)

        @pl.loop(1, R)
        def _(k):
            peer = away(k)
            remote(b_row.at[it, row], b_row.at[it, peer], b_ss.at[it, peer], b_rs.at[it, peer], peer, col).wait_recv()
        split(b_row, lhs_r, R)

        for s in range(C):
            g = row * C + s
            own_row, own_col = lax.rem(g, R), g // R
            here = jnp.logical_and(own_row == row, own_col == col)

            @pl.when(jnp.logical_not(here))
            def _():
                remote(b_row.at[it, row], b_left.at[it, s], bl_ss.at[it, s], bl_rs.at[it, s], own_row, own_col).wait_recv()
        split(b_left, lhs_l, C)

        lacc[...] = jnp.zeros_like(lacc)

        @pl.loop(0, C)
        def _(s):
            g = row * C + s
            own_row, own_col = lax.rem(g, R), g // R
            at = pl.multiple_of(s * chunk, chunk)
            part = kb[pl.ds(at, chunk), :]
            right = lax.dot_general(lhs_r[...], part, (((1,), (1,)), ((), ())), preferred_element_type=f32)
            c_rsend[it, s] = right[:8] + right[8:]
            here = jnp.logical_and(own_row == row, own_col == col)

            @pl.when(here)
            def _():
                c_rrecv[it, col] = c_rsend[it, s]

            @pl.when(jnp.logical_not(here))
            def _():
                remote(c_rsend.at[it, s], c_rrecv.at[it, col], cr_ss.at[it, s], cr_rs.at[it, col], own_row, own_col).start()
            left = jnp.dot(lhs_l[:, pl.ds(at, chunk)], part, preferred_element_type=f32)
            lacc[...] += left[:8] + left[8:]

        for j in range(R):
            c_lsend[it, j] = lacc[:, j * chunk:(j + 1) * chunk]
        c_lrecv[it, row] = c_lsend[it, row]

        @pl.loop(1, R)
        def _(k):
            peer = away(k)
            remote(c_lsend.at[it, peer], c_lrecv.at[it, row], cl_ss.at[it, peer], cl_rs.at[it, row], peer, col).start()

        for j in range(C):
            here = jnp.logical_and(owner_row == row, col == j)

            @pl.when(jnp.logical_not(here))
            def _():
                remote(c_rsend.at[it, j], c_rrecv.at[it, j], cr_ss.at[it, j], cr_rs.at[it, j], owner_row, j).wait_recv()

        @pl.loop(1, R)
        def _(k):
            peer = away(k)
            remote(c_lsend.at[it, peer], c_lrecv.at[it, peer], cl_ss.at[it, peer], cl_rs.at[it, peer], peer, col).wait_recv()
        zr = c_rrecv[it, 0]
        for j in range(1, C):
            zr = zr + c_rrecv[it, j]
        zl = c_lrecv[it, 0]
        for j in range(1, R):
            zl = zl + c_lrecv[it, j]
        sub = lax.broadcasted_iota(jnp.int32, (stack, chunk), 0)
        d_row[it, row] = jnp.where(sub < count, zr, zl)

        @pl.loop(1, R)
        def _(k):
            peer = away(k)
            remote(d_row.at[it, row], d_row.at[it, row], d_ss.at[it, peer], d_rs.at[it, row], peer, col).start()

        @pl.loop(1, R)
        def _(k):
            peer = away(k)
            remote(d_row.at[it, row], d_row.at[it, peer], d_ss.at[it, peer], d_rs.at[it, peer], peer, col).wait_recv()

        def e_copy(b):
            return remote(e_send.at[it, b], e_recv.at[it, b], e_ss.at[it, b], e_rs.at[it, b], row, mate)

        def y_copy(b, k, sender):
            other = lax.rem(ypos + k, Y)
            return remote(
                y_all.at[it, ypos, b], y_all.at[it, sender, b], y_ss.at[it, k, b], y_rs.at[it, sender, b],
                row, other * 2 + core,
            )

        def g_copy(b, sender):
            return remote(g_all.at[it, core, b], g_all.at[it, sender, b], g_ss.at[it, b], g_rs.at[it, sender, b], row, mate)

        own = pl.ds(pl.multiple_of(core * half, half), half)
        rest = pl.ds(pl.multiple_of((1 - core) * half, half), half)

        def backward(b):
            for j in range(R):
                at = slice(j * chunk, (j + 1) * chunk)
                z = d_row[it, j, pl.ds(b, 1), :]
                wbuf[:, at] = (cond[:, at].astype(f32) * z).astype(bf16)
            total = jnp.zeros((nc, nv), f32)
            for j in range(R):
                at = slice(j * chunk, (j + 1) * chunk)
                total = total + lax.dot_general(
                    wbuf[:, at], panel[:, :, at].reshape(nv, chunk), (((1,), (1,)), ((), ())),
                    preferred_element_type=f32,
                )
            img[b] = total
            e_send[it, b] = img[b, rest, :].astype(bf16)
            e_copy(b).start()

        def cross(b):
            e_copy(b).wait_recv()
            y_all[it, ypos, b] = (img[b, own, :] + e_recv[it, b].astype(f32)).astype(bf16)
            for k in range(1, Y):
                y_copy(b, k, ypos).start()

        def finish(b):
            for k in range(1, Y):
                y_copy(b, k, lax.rem(ypos + k, Y)).wait_recv()
            total = y_all[it, 0, b].astype(f32)
            for k in range(1, Y):
                total = total + y_all[it, k, b].astype(f32)
            g_all[it, core, b] = total.astype(bf16)
            g_copy(b, core).start()

        @pl.loop(0, stack)
        def _(b):
            backward(b)

            @pl.when(b >= 1)
            def _():
                cross(b - 1)

        cross(stack - 1)

        @pl.loop(0, stack)
        def _(b):
            finish(b)

        @pl.loop(0, stack)
        def _(b):
            g_copy(b, 1 - core).wait_recv()
            for h in range(2):
                rows = slice(h * half, (h + 1) * half)
                img[b, rows, :] = energy[rows, :] * xs[it, b, rows, :] + g_all[it, h, b].astype(f32)

        for b in range(count):
            def add(g, acc):
                at = pl.ds(pl.multiple_of(g * 8, 8), 8)
                ir, il = img[b, at, :], img[count + b, at, :]
                q, p = xs[it, b, at, :], xs[it, count + b, at, :]
                if it == 0:
                    pairs = [(p, ir), (il, ir), (il, q), (p, q), (ir, ir), (q, q), (ir, q), (il, il), (p, p), (il, p)]
                else:
                    qo, po = xs[it - 1, b, at, :], xs[it - 1, count + b, at, :]
                    pairs = [
                        (p, ir), (il, ir), (il, q), (p, q), (ir, ir), (q, q), (ir, q), (il, il), (p, p), (il, p),
                        (po, ir), (qo, il), (p, qo), (po, q), (po, qo), (qo, qo), (ir, qo), (q, qo), (po, po), (il, po), (p, po),
                    ]
                out = []
                for old, (u, w) in zip(acc, pairs):
                    prod = u * w
                    out.append(old + prod[:, :128] + prod[:, 128:])
                return tuple(out)
            n_terms = 10 if it == 0 else 21
            acc = lax.fori_loop(0, nc // 8, add, tuple(jnp.zeros((8, 128), f32) for _ in range(n_terms)))
            for t in range(n_terms):
                terms[b, t:t + 1, :] = jnp.sum(acc[t], axis=0, keepdims=True)
            terms[b, n_terms:TERMS, :] = jnp.zeros((TERMS - n_terms, 128), f32)
        lanes = lax.broadcasted_iota(jnp.int32, (TERMS, 128), 1)
        tile = jnp.zeros((TERMS, 128), f32)
        for b in range(count):
            tile = tile + jnp.where(lanes == b, jnp.sum(terms[b], axis=1, keepdims=True), 0.0)
        t_all[it + 1, row] = tile
        table_start(it + 1)
        table = table_wait(it + 1)
        T = [table[t:t + 1, :] for t in range(TERMS)]
        alpha = T[0]
        cross_term = T[1] - alpha * T[2] - alpha * alpha + alpha * alpha * T[3]
        right_sq = T[4] + alpha * alpha * T[5] - 2.0 * alpha * T[6]
        left_sq = T[7] + alpha * alpha * T[8] - 2.0 * alpha * T[9]
        if it:
            mu, nu = T[10], T[11]
            cross_term = (
                cross_term - mu * nu + alpha * mu * T[12] - nu * mu + nu * alpha * T[13] + nu * mu * T[14]
            )
            right_sq = right_sq + mu * mu * T[15] - 2.0 * mu * T[16] + 2.0 * alpha * mu * T[17]
            left_sq = left_sq + nu * nu * T[18] - 2.0 * nu * T[19] + 2.0 * alpha * nu * T[20]
        beta = jnp.sqrt(jnp.maximum(cross_term, 0.25 * jnp.sqrt(right_sq * left_sq)))
        out_c[2 * it:2 * it + 1, :] = alpha
        out_c[2 * it + 1:2 * it + 2, :] = beta
        inverse = 1.0 / beta
        for b in range(count):
            one = slice(b, b + 1)
            r = img[b] - alpha[:, one] * xs[it, b]
            s = img[count + b] - alpha[:, one] * xs[it, count + b]
            if it:
                r = r - mu[:, one] * xs[it - 1, b]
                s = s - nu[:, one] * xs[it - 1, count + b]
            r = r * inverse[:, one]
            s = s * inverse[:, one]
            if it + 1 == ITERS:
                out_r[b] = r
                out_l[b] = s
            else:
                xs[it + 1, b] = r
                xs[it + 1, count + b] = s
                xb[b] = r.astype(bf16)
                xb[count + b] = s.astype(bf16)

        @pl.loop(1, R)
        def _(k):
            peer = away(k)
            remote(a_send.at[it, peer], a_recv.at[it, row], a_ss.at[it, peer], a_rs.at[it, row], peer, col).wait_send()
            remote(b_row.at[it, row], b_row.at[it, row], b_ss.at[it, peer], b_rs.at[it, row], peer, col).wait_send()
            remote(c_lsend.at[it, peer], c_lrecv.at[it, row], cl_ss.at[it, peer], cl_rs.at[it, row], peer, col).wait_send()
            remote(d_row.at[it, row], d_row.at[it, row], d_ss.at[it, peer], d_rs.at[it, row], peer, col).wait_send()
            remote(t_all.at[it + 1, row], t_all.at[it + 1, row], t_ss.at[it + 1, peer], t_rs.at[it + 1, row], peer, col).wait_send()

        for j in range(C):
            here = jnp.logical_and(owner_row == row, col == j)

            @pl.when(jnp.logical_not(here))
            def _():
                remote(b_row.at[it, row], b_left.at[it, slot_left], bl_ss.at[it, j], bl_rs.at[it, slot_left], owner_row, j).wait_send()

            g = row * C + j
            own_row, own_col = lax.rem(g, R), g // R
            there = jnp.logical_and(own_row == row, own_col == col)

            @pl.when(jnp.logical_not(there))
            def _():
                remote(c_rsend.at[it, j], c_rrecv.at[it, col], cr_ss.at[it, j], cr_rs.at[it, col], own_row, own_col).wait_send()

        @pl.loop(0, stack)
        def _(b):
            e_copy(b).wait_send()
            for k in range(1, Y):
                y_copy(b, k, ypos).wait_send()
            g_copy(b, core).wait_send()

    @pl.loop(1, R)
    def _(k):
        peer = away(k)
        remote(t_all.at[0, row], t_all.at[0, row], t_ss.at[0, peer], t_rs.at[0, row], peer, col).wait_send()

    @pl.loop(0, L)
    def _(z):
        block = z * 2 + side
        blk(block, p_x, pair).wait_send()

        @pl.when(jnp.logical_and(z <= line, line + 1 < L))
        def _():
            blk(block, p_up, row + 2).wait_send()

        @pl.when(jnp.logical_and(z >= line, line >= 1))
        def _():
            blk(block, p_dn, row - 2).wait_send()


def fused(mesh, start_vec, cond_orb, val_orb, kernel, cond_energy, val_energy):
    R, C = mesh.shape["row"], mesh.shape["col"]
    count, nc, nv = start_vec.shape
    stack = 2 * count
    half = nc // 2
    span_row, span_col = kernel.shape
    vs = val_orb.shape[0]
    chunk = span_row // C
    Y = C // 2
    f32, bf16 = jnp.float32, jnp.bfloat16
    V = pltpu.VMEM
    D = pltpu.SemaphoreType.DMA
    energy = cond_energy[:, None] - val_energy[None, :]
    vm = pl.BlockSpec(memory_space=pltpu.VMEM)
    scratch = [
        V((R, vs, span_col), bf16),
        V((span_row, span_col), bf16),
        V((2, ROWS_K, span_col), f32),
        V((ITERS, stack, nc, nv), f32),
        V((stack, nc, nv), bf16),
        V((stack, nc, nv), f32),
        V((nc, span_col), bf16),
        V((2 * stack, span_col), bf16),
        V((2 * stack, span_row), bf16),
        V((stack, span_col), f32),
        V((count, TERMS, 128), f32),
        V((ITERS, R, stack, chunk), f32),
        V((ITERS, R, stack, chunk), f32),
        V((ITERS, R, stack, chunk), f32),
        V((ITERS, C, stack, chunk), f32),
        V((ITERS, C, stack, chunk), f32),
        V((ITERS, C, stack, chunk), f32),
        V((ITERS, R, stack, chunk), f32),
        V((ITERS, R, stack, chunk), f32),
        V((ITERS, R, stack, chunk), f32),
        V((ITERS, stack, half, nv), bf16),
        V((ITERS, stack, half, nv), bf16),
        V((ITERS, Y, stack, half, nv), bf16),
        V((ITERS, 2, stack, half, nv), bf16),
        V((ITERS + 1, R, TERMS, 128), f32),
        D((2,)),
        D((R,)), D((R,)), D((R,)), D((R,)),
        D((ITERS, R)), D((ITERS, R)),
        D((ITERS, R)), D((ITERS, R)),
        D((ITERS, C)), D((ITERS, C)),
        D((ITERS, C)), D((ITERS, C)),
        D((ITERS, R)), D((ITERS, R)),
        D((ITERS, R)), D((ITERS, R)),
        D((ITERS, stack)), D((ITERS, stack)),
        D((ITERS, Y, stack)), D((ITERS, Y, stack)),
        D((ITERS, stack)), D((ITERS, 2, stack)),
        D((ITERS + 1, R)), D((ITERS + 1, R)),
    ]
    right, left, coefs = pl.pallas_call(
        functools.partial(body_kernel, R, C),
        out_shape=(
            jax.ShapeDtypeStruct((count, nc, nv), f32),
            jax.ShapeDtypeStruct((count, nc, nv), f32),
            jax.ShapeDtypeStruct((2 * ITERS, 128), f32),
        ),
        in_specs=[vm, vm, vm, pl.BlockSpec(memory_space=pl.ANY), vm],
        out_specs=(vm, vm, vm),
        scratch_shapes=scratch,
        compiler_params=pltpu.CompilerParams(
            collective_id=0, has_side_effects=True, vmem_limit_bytes=62 * 2**20
        ),
    )(start_vec, cond_orb, val_orb, kernel, energy)
    return right, left, coefs[:, :count].T


def solution(mesh):
    in_specs = (
        P(None, "row", None),
        P("row", "col"),
        P("row", "col"),
        P("row", "col"),
        P("row"),
        P(),
    )
    out_specs = (P(None, "row", None), P(None, "row", None), P())

    def run(*arrays):
        body = fused if fits(mesh, *arrays) else shards
        return jax.shard_map(
            functools.partial(body, mesh) if body is fused else body,
            mesh=mesh,
            in_specs=in_specs,
            out_specs=out_specs,
            check_vma=False,
        )(*arrays)

    return run
```

```python
import functools

import jax
import jax.numpy as jnp
from jax import lax
from jax.experimental import pallas as pl
from jax.experimental.pallas import tpu as pltpu
from jax.sharding import PartitionSpec as P

ITERS = 2


def inner_local(first, second):
    return jnp.sum(first * second, axis=(1, 2))


def shards(start_vec, cond_orb, val_orb, kernel, cond_energy, val_energy):
    count = start_vec.shape[0]
    row_place = lax.axis_index("row")
    col_place = lax.axis_index("col")
    span_row = kernel.shape[0]
    span_col = kernel.shape[1]
    panel = lax.all_gather(val_orb, "row", axis=0, tiled=True)
    cond_f = cond_orb.astype(jnp.float32)
    energy = cond_energy[:, None] - val_energy[None, :]

    def row_total(values):
        return lax.psum(values, "row")

    def col_total(values):
        return lax.psum(values, "col")

    def reduce_dots(terms):
        return row_total(terms)

    (norm_sq,) = reduce_dots((inner_local(start_vec, start_vec),))
    right = start_vec / jnp.sqrt(norm_sq)[:, None, None]
    left = right
    right_old = jnp.zeros_like(right)
    left_old = jnp.zeros_like(left)
    record = []
    for step in range(ITERS):
        stack = jnp.concatenate([right, left], axis=0)
        rounded = stack.astype(jnp.bfloat16)
        paired = jnp.einsum("bcv,vn->bcn", rounded, panel, preferred_element_type=jnp.float32)
        partial_value = jnp.sum(paired * cond_f[None], axis=1)
        folded = row_total(partial_value)
        right_coeff = folded[:count]
        left_coeff = folded[count:]
        left_all = lax.all_gather(left_coeff, "col", axis=1, tiled=True)
        left_rows = lax.dynamic_slice_in_dim(left_all, row_place * span_row, span_row, 1)
        right_part = jnp.einsum(
            "bn,mn->bm",
            right_coeff,
            kernel,
            precision=lax.Precision.HIGHEST,
            preferred_element_type=jnp.float32,
        )
        left_part = jnp.einsum(
            "bm,mn->bn",
            left_rows,
            kernel,
            precision=lax.Precision.HIGHEST,
            preferred_element_type=jnp.float32,
        )
        right_zed = col_total(right_part)
        left_zed = row_total(left_part)
        right_all = lax.all_gather(right_zed, "row", axis=1, tiled=True)
        right_cols = lax.dynamic_slice_in_dim(right_all, col_place * span_col, span_col, 1)
        zed = jnp.concatenate([right_cols, left_zed], axis=0)
        weighted = (cond_f[None] * zed[:, None, :]).astype(jnp.bfloat16)
        image_terms = jnp.einsum("bcn,vn->bcv", weighted, panel, preferred_element_type=jnp.float32)
        kernel_part = col_total(image_terms)
        images = energy[None] * stack + kernel_part
        image_r = images[:count]
        image_l = images[count:]
        table = reduce_dots(
            (
                inner_local(left, image_r),
                inner_local(left_old, image_r),
                inner_local(right_old, image_l),
                inner_local(image_l, image_r),
                inner_local(image_l, right),
                inner_local(left, right),
                inner_local(left, right_old),
                inner_local(left_old, right),
                inner_local(left_old, right_old),
                inner_local(image_r, image_r),
                inner_local(right, right),
                inner_local(right_old, right_old),
                inner_local(image_r, right),
                inner_local(image_r, right_old),
                inner_local(right, right_old),
                inner_local(image_l, image_l),
                inner_local(left, left),
                inner_local(left_old, left_old),
                inner_local(image_l, left),
                inner_local(image_l, left_old),
                inner_local(left, left_old),
            )
        )
        alpha, mu_co, nu_co = (table[0], table[1], table[2])
        cross = (
            table[3]
            - alpha * table[4]
            - mu_co * nu_co
            - alpha * alpha
            + alpha * alpha * table[5]
            + alpha * mu_co * table[6]
            - nu_co * mu_co
            + nu_co * alpha * table[7]
            + nu_co * mu_co * table[8]
        )
        right_sq = (
            table[9]
            + alpha * alpha * table[10]
            + mu_co * mu_co * table[11]
            - 2.0 * alpha * table[12]
            - 2.0 * mu_co * table[13]
            + 2.0 * alpha * mu_co * table[14]
        )
        left_sq = (
            table[15]
            + alpha * alpha * table[16]
            + nu_co * nu_co * table[17]
            - 2.0 * alpha * table[18]
            - 2.0 * nu_co * table[19]
            + 2.0 * alpha * nu_co * table[20]
        )
        resid_r = image_r - alpha[:, None, None] * right - mu_co[:, None, None] * right_old
        resid_l = image_l - alpha[:, None, None] * left - nu_co[:, None, None] * left_old
        bound = jnp.maximum(cross, 0.25 * jnp.sqrt(right_sq * left_sq))
        beta = jnp.sqrt(bound)
        right_old, left_old = (right, left)
        right = resid_r / beta[:, None, None]
        left = resid_l / beta[:, None, None]
        record.append(alpha)
        record.append(beta)
    joined = jnp.concatenate([right, left], axis=0)
    return (joined[:count], joined[count:], jnp.stack(record, axis=1))


MESH = pl.DeviceIdType.MESH
TERMS = 24
ROWS_K = 256


def fits(mesh, start_vec, cond_orb, val_orb, kernel, cond_energy, val_energy):
    R, C = mesh.shape["row"], mesh.shape["col"]
    points = kernel.shape[0]
    chunk = points // (R * C)
    local = cond_orb.shape[0] // R
    kernel_bytes = 2 * (points // R) * (points // C)
    return (
        start_vec.shape[0] == 4
        and R % 2 == 0
        and C == 4
        and chunk % ROWS_K == 0
        and local % 32 == 0
        and (val_orb.shape[0] // R) % 16 == 0
        and val_orb.shape[0] == 256
        and kernel_bytes <= 16 * 2**20
    )


def body_kernel(
    R, C,
    start, cond, val, kmat, energy,
    out_r, out_l, out_c,
    panel, kb, kf, xs, xb, img, wbuf, lhs_r, lhs_l, terms,
    a0_send, a0_recv, a1_send, a1_recv, b_row, b_own, b_left, c_rsend, c_rrecv, c_lsend, c_lrecv, d_row,
    e_send, e_recv, y_all, g_all, t_all,
    k_sem, p_up, p_dn, p_x, p_recv,
    a_ss, a_rs, b_ss, b_rs, bl_ss, bl_rs, cr_ss, cr_rs, cl_ss, cl_rs, d_ss, d_rs,
    e_ss, e_rs, y_ss, y_rs, g_ss, g_rs, t_ss, t_rs,
):
    row = lax.axis_index("row")
    col = lax.axis_index("col")
    count = start.shape[0]
    stack = 2 * count
    nc = start.shape[1]
    nv = start.shape[2]
    half = nc // 2
    chunk = a0_send.shape[-1]
    span_row = kb.shape[0]
    span_col = kb.shape[1]
    Y = C // 2
    core = lax.rem(col, 2)
    ypos = col // 2
    mate = ypos * 2 + 1 - core
    f32, bf16 = jnp.float32, jnp.bfloat16
    mine = col * R + row
    owner_row = mine // C
    slot_left = lax.rem(mine, C)

    def remote(src, dst, ss, rs, to_row, to_col):
        return pltpu.make_async_remote_copy(
            src_ref=src, dst_ref=dst, send_sem=ss, recv_sem=rs,
            device_id=(to_row, to_col), device_id_type=MESH,
        )

    def away(k):
        return lax.rem(row + k, R)

    barrier = pltpu.get_barrier_semaphore()

    @pl.loop(1, R * C)
    def _(k):
        flat = lax.rem(row * C + col + k, R * C)
        pl.semaphore_signal(barrier, inc=1, device_id=(flat // C, lax.rem(flat, C)), device_id_type=MESH)

    def kcopy(i, slot):
        return pltpu.make_async_copy(
            kmat.at[pl.ds(i * ROWS_K, ROWS_K), :], kf.at[slot], k_sem.at[slot]
        )

    kcopy(0, 0).start()
    kcopy(1, 1).start()
    panel[row] = val[...]

    for b in range(count):
        sq = jnp.sum(start[b] * start[b], axis=0, keepdims=True)
        terms[b, 0:1, :] = sq[:, :128] + sq[:, 128:]
    lane = lax.broadcasted_iota(jnp.int32, (8, 128), 1)
    tile = jnp.zeros((8, 128), f32)
    for b in range(count):
        total = jnp.sum(terms[b, 0:1, :], axis=1, keepdims=True)
        tile = tile + jnp.where(lane == b, total, 0.0)
    t_all[0, row] = tile

    pl.semaphore_wait(barrier, R * C - 1)

    def table_start(i):
        @pl.loop(1, R)
        def _(k):
            peer = away(k)
            remote(t_all.at[i, row], t_all.at[i, row], t_ss.at[i, peer], t_rs.at[i, row], peer, col).start()

    def table_wait(i):
        @pl.loop(1, R)
        def _(k):
            peer = away(k)
            remote(t_all.at[i, row], t_all.at[i, peer], t_ss.at[i, peer], t_rs.at[i, peer], peer, col).wait_recv()
        total = t_all[i, 0]
        for k in range(1, R):
            total = total + t_all[i, k]
        return total

    table_start(0)

    L = R // 2
    line = row // 2
    side = lax.rem(row, 2)
    pair = line * 2 + 1 - side

    def blk(block, sem, to_row):
        return remote(panel.at[block], panel.at[block], sem.at[block], p_recv.at[block], to_row, col)

    def pass_on(block, up, down):
        if up:
            @pl.when(line + 1 < L)
            def _():
                blk(block, p_up, row + 2).start()
        if down:
            @pl.when(line >= 1)
            def _():
                blk(block, p_dn, row - 2).start()
        blk(block, p_x, pair).start()

    pass_on(row, True, True)

    n_k = span_row // ROWS_K

    def take_k(i):
        slot = lax.rem(i, 2)
        kcopy(i, slot).wait()
        base = pl.multiple_of(i * ROWS_K, ROWS_K)

        @pl.loop(0, ROWS_K // 16)
        def _(g):
            at = pl.multiple_of(g * 16, 16)
            kb[pl.ds(pl.multiple_of(base + at, 16), 16), :] = kf[slot, pl.ds(at, 16), :].astype(bf16)

        @pl.when(i + 2 < n_k)
        def _():
            kcopy(i + 2, slot).start()

    per = n_k // L
    for d in range(L):
        @pl.loop(d * per, n_k if d == L - 1 else (d + 1) * per)
        def _(i):
            take_k(i)
        if d == 0:
            total = table_wait(0)
            scale = 1.0 / jnp.sqrt(total[0:1, :])
            for b in range(count):
                q = start[b] * scale[:, b:b + 1]
                xs[0, b] = q
                xs[0, count + b] = q
                xb[b] = q.astype(bf16)
        if d + 1 < L:
            @pl.when(line - (d + 1) >= 0)
            def _():
                block = row - 2 * (d + 1)
                blk(block, p_x, pair).wait_recv()
                pass_on(block, True, False)

            @pl.when(line + (d + 1) < L)
            def _():
                block = row + 2 * (d + 1)
                blk(block, p_x, pair).wait_recv()
                pass_on(block, False, True)

    @pl.loop(0, L)
    def _(z):
        blk(z * 2 + 1 - side, p_x, pair).wait_recv()

    for it in range(ITERS):
        wide = count if it == 0 else stack
        a_send, a_recv = (a0_send, a0_recv) if it == 0 else (a1_send, a1_recv)

        @pl.loop(1, R + 1)
        def _(k):
            peer = away(k)
            at = pl.multiple_of(peer * chunk, chunk)
            block = panel[:, :, pl.ds(at, chunk)].reshape(nv, chunk)
            weight = cond[:, pl.ds(at, chunk)].astype(f32)
            for b in range(wide):
                paired = jnp.dot(xb[b], block, preferred_element_type=f32)
                value = jnp.sum(paired * weight, axis=0, keepdims=True)
                a_send[peer, b:b + 1, :] = value

            @pl.when(k < R)
            def _():
                remote(a_send.at[peer], a_recv.at[row], a_ss.at[it, peer], a_rs.at[it, row], peer, col).start()

        @pl.loop(1, R)
        def _(k):
            peer = away(k)
            remote(a_send.at[peer], a_recv.at[peer], a_ss.at[it, peer], a_rs.at[it, peer], peer, col).wait_recv()
        a_recv[row] = a_send[row]
        coeff = a_recv[0]
        for k in range(1, R):
            coeff = coeff + a_recv[k]
        right_coeff = coeff[:count]
        left_coeff = coeff if it == 0 else coeff[count:]

        b_row[it, row] = right_coeff
        b_own[it] = left_coeff
        for j in range(C):
            here = jnp.logical_and(owner_row == row, col == j)

            @pl.when(here)
            def _():
                b_left[it, slot_left] = left_coeff

            @pl.when(jnp.logical_not(here))
            def _():
                remote(b_own.at[it], b_left.at[it, slot_left], bl_ss.at[it, j], bl_rs.at[it, slot_left], owner_row, j).start()

        @pl.loop(1, R)
        def _(k):
            peer = away(k)
            remote(b_row.at[it, row], b_row.at[it, row], b_ss.at[it, peer], b_rs.at[it, row], peer, col).start()

        def split(ref, dst, pieces):
            for j in range(pieces):
                piece = ref[it, j]
                high = piece.astype(bf16).astype(f32)
                dst[:, j * chunk:(j + 1) * chunk] = jnp.concatenate([high, piece - high], axis=0).astype(bf16)

        for s in range(C):
            g = row * C + s
            own_row, own_col = lax.rem(g, R), g // R
            here = jnp.logical_and(own_row == row, own_col == col)

            @pl.when(jnp.logical_not(here))
            def _():
                remote(b_own.at[it], b_left.at[it, s], bl_ss.at[it, s], bl_rs.at[it, s], own_row, own_col).wait_recv()
        split(b_left, lhs_l, C)

        @pl.loop(1, R + 1)
        def _(k):
            peer = away(k)
            at = pl.multiple_of(peer * chunk, chunk)
            left = jnp.dot(lhs_l[...], kb[:, pl.ds(at, chunk)], preferred_element_type=f32)
            c_lsend[it, peer] = left[:count] + left[count:]

            @pl.when(k < R)
            def _():
                remote(c_lsend.at[it, peer], c_lrecv.at[it, row], cl_ss.at[it, peer], cl_rs.at[it, row], peer, col).start()

        c_lrecv[it, row] = c_lsend[it, row]

        @pl.loop(1, R)
        def _(k):
            peer = away(k)
            remote(b_row.at[it, row], b_row.at[it, peer], b_ss.at[it, peer], b_rs.at[it, peer], peer, col).wait_recv()
        split(b_row, lhs_r, R)

        @pl.loop(0, C)
        def _(s):
            g = row * C + s
            own_row, own_col = lax.rem(g, R), g // R
            part = kb[pl.ds(pl.multiple_of(s * chunk, chunk), chunk), :]
            right = lax.dot_general(lhs_r[...], part, (((1,), (1,)), ((), ())), preferred_element_type=f32)
            c_rsend[it, s] = right[:count] + right[count:]
            here = jnp.logical_and(own_row == row, own_col == col)

            @pl.when(here)
            def _():
                c_rrecv[it, col] = c_rsend[it, s]

            @pl.when(jnp.logical_not(here))
            def _():
                remote(c_rsend.at[it, s], c_rrecv.at[it, col], cr_ss.at[it, s], cr_rs.at[it, col], own_row, own_col).start()

        for j in range(C):
            here = jnp.logical_and(owner_row == row, col == j)

            @pl.when(jnp.logical_not(here))
            def _():
                remote(c_rsend.at[it, j], c_rrecv.at[it, j], cr_ss.at[it, j], cr_rs.at[it, j], owner_row, j).wait_recv()

        @pl.loop(1, R)
        def _(k):
            peer = away(k)
            remote(c_lsend.at[it, peer], c_lrecv.at[it, peer], cl_ss.at[it, peer], cl_rs.at[it, peer], peer, col).wait_recv()
        zr = c_rrecv[it, 0]
        for j in range(1, C):
            zr = zr + c_rrecv[it, j]
        zl = c_lrecv[it, 0]
        for j in range(1, R):
            zl = zl + c_lrecv[it, j]
        d_row[it, row] = jnp.concatenate([zr, zl], axis=0)

        @pl.loop(1, R)
        def _(k):
            peer = away(k)
            remote(d_row.at[it, row], d_row.at[it, row], d_ss.at[it, peer], d_rs.at[it, row], peer, col).start()

        @pl.loop(1, R)
        def _(k):
            peer = away(k)
            remote(d_row.at[it, row], d_row.at[it, peer], d_ss.at[it, peer], d_rs.at[it, peer], peer, col).wait_recv()

        def e_copy(b):
            return remote(e_send.at[it, b], e_recv.at[it, b], e_ss.at[it, b], e_rs.at[it, b], row, mate)

        def y_copy(b, k, sender):
            other = lax.rem(ypos + k, Y)
            return remote(
                y_all.at[it, ypos, b], y_all.at[it, sender, b], y_ss.at[it, k, b], y_rs.at[it, sender, b],
                row, other * 2 + core,
            )

        def g_copy(b, sender):
            return remote(g_all.at[it, core, b], g_all.at[it, sender, b], g_ss.at[it, b], g_rs.at[it, sender, b], row, mate)

        own = pl.ds(pl.multiple_of(core * half, half), half)
        rest = pl.ds(pl.multiple_of((1 - core) * half, half), half)

        def backward(b):
            for j in range(R):
                at = slice(j * chunk, (j + 1) * chunk)
                z = d_row[it, j, pl.ds(b, 1), :]
                wbuf[:, at] = (cond[:, at].astype(f32) * z).astype(bf16)
            total = jnp.zeros((nc, nv), f32)
            for j in range(R):
                at = slice(j * chunk, (j + 1) * chunk)
                total = total + lax.dot_general(
                    wbuf[:, at], panel[:, :, at].reshape(nv, chunk), (((1,), (1,)), ((), ())),
                    preferred_element_type=f32,
                )
            img[b] = total
            e_send[it, b] = img[b, rest, :]
            e_copy(b).start()

        def cross(b):
            e_copy(b).wait_recv()
            y_all[it, ypos, b] = (img[b, own, :] + e_recv[it, b]).astype(bf16)
            for k in range(1, Y):
                y_copy(b, k, ypos).start()

        def finish(b):
            for k in range(1, Y):
                y_copy(b, k, lax.rem(ypos + k, Y)).wait_recv()
            total = y_all[it, 0, b].astype(f32)
            for k in range(1, Y):
                total = total + y_all[it, k, b].astype(f32)
            g_all[it, core, b] = total
            g_copy(b, core).start()

        @pl.loop(0, stack)
        def _(b):
            backward(b)

            @pl.when(b >= 1)
            def _():
                cross(b - 1)

        cross(stack - 1)

        @pl.loop(0, stack)
        def _(b):
            finish(b)

        @pl.loop(0, stack)
        def _(b):
            g_copy(b, 1 - core).wait_recv()
            for h in range(2):
                rows = slice(h * half, (h + 1) * half)
                img[b, rows, :] = energy[rows, :] * xs[it, b, rows, :] + g_all[it, h, b]

        for b in range(count):
            def add(g, acc):
                at = pl.ds(pl.multiple_of(g * 8, 8), 8)
                ir, il = img[b, at, :], img[count + b, at, :]
                q, p = xs[it, b, at, :], xs[it, count + b, at, :]
                if it == 0:
                    pairs = [(q, ir), (il, ir), (il, q), (q, q), (ir, ir), (il, il)]
                else:
                    qo, po = xs[it - 1, b, at, :], xs[it - 1, count + b, at, :]
                    pairs = [
                        (p, ir), (il, ir), (il, q), (p, q), (ir, ir), (q, q), (ir, q), (il, il), (p, p), (il, p),
                        (po, ir), (qo, il), (p, qo), (po, q), (po, qo), (qo, qo), (ir, qo), (q, qo), (po, po), (il, po), (p, po),
                    ]
                out = []
                for old, (u, w) in zip(acc, pairs):
                    prod = u * w
                    out.append(old + prod[:, :128] + prod[:, 128:])
                return tuple(out)
            n_terms = 6 if it == 0 else 21
            acc = lax.fori_loop(0, nc // 8, add, tuple(jnp.zeros((8, 128), f32) for _ in range(n_terms)))
            for t in range(n_terms):
                terms[b, t:t + 1, :] = jnp.sum(acc[t], axis=0, keepdims=True)
            terms[b, n_terms:TERMS, :] = jnp.zeros((TERMS - n_terms, 128), f32)
        tile = jnp.zeros((8, 128), f32)
        groups = 1 if it == 0 else TERMS // 8
        for b in range(count):
            sums = jnp.sum(terms[b], axis=1, keepdims=True)
            for g in range(groups):
                tile = tile + jnp.where(lane == count * g + b, sums[8 * g:8 * g + 8], 0.0)
        t_all[it + 1, row] = tile
        table_start(it + 1)
        table = table_wait(it + 1)
        packs = [table] + [pltpu.roll(table, 128 - count * g, 1) for g in range(1, groups)]
        T = [packs[t // 8][t % 8:t % 8 + 1, :] for t in range(8 * groups)]
        if it == 0:
            T = [T[0], T[1], T[2], T[3], T[4], T[3], T[0], T[5], T[3], T[2]]
        alpha = T[0]
        cross_term = T[1] - alpha * T[2] - alpha * alpha + alpha * alpha * T[3]
        right_sq = T[4] + alpha * alpha * T[5] - 2.0 * alpha * T[6]
        left_sq = T[7] + alpha * alpha * T[8] - 2.0 * alpha * T[9]
        if it:
            mu, nu = T[10], T[11]
            cross_term = (
                cross_term - mu * nu + alpha * mu * T[12] - nu * mu + nu * alpha * T[13] + nu * mu * T[14]
            )
            right_sq = right_sq + mu * mu * T[15] - 2.0 * mu * T[16] + 2.0 * alpha * mu * T[17]
            left_sq = left_sq + nu * nu * T[18] - 2.0 * nu * T[19] + 2.0 * alpha * nu * T[20]
        beta = jnp.sqrt(jnp.maximum(cross_term, 0.25 * jnp.sqrt(right_sq * left_sq)))
        out_c[2 * it:2 * it + 1, :] = alpha
        out_c[2 * it + 1:2 * it + 2, :] = beta
        inverse = 1.0 / beta
        for b in range(count):
            one = slice(b, b + 1)
            r = img[b] - alpha[:, one] * xs[it, b]
            s = img[count + b] - alpha[:, one] * xs[it, count + b]
            if it:
                r = r - mu[:, one] * xs[it - 1, b]
                s = s - nu[:, one] * xs[it - 1, count + b]
            if it + 1 == ITERS:
                out_r[b] = r
                out_l[b] = s
            else:
                r = r * inverse[:, one]
                s = s * inverse[:, one]
                xs[it + 1, b] = r
                xs[it + 1, count + b] = s
                xb[b] = r.astype(bf16)
                xb[count + b] = s.astype(bf16)

        @pl.loop(1, R)
        def _(k):
            peer = away(k)
            remote(a_send.at[peer], a_recv.at[row], a_ss.at[it, peer], a_rs.at[it, row], peer, col).wait_send()
            remote(b_row.at[it, row], b_row.at[it, row], b_ss.at[it, peer], b_rs.at[it, row], peer, col).wait_send()
            remote(c_lsend.at[it, peer], c_lrecv.at[it, row], cl_ss.at[it, peer], cl_rs.at[it, row], peer, col).wait_send()
            remote(d_row.at[it, row], d_row.at[it, row], d_ss.at[it, peer], d_rs.at[it, row], peer, col).wait_send()
            remote(t_all.at[it + 1, row], t_all.at[it + 1, row], t_ss.at[it + 1, peer], t_rs.at[it + 1, row], peer, col).wait_send()

        for j in range(C):
            here = jnp.logical_and(owner_row == row, col == j)

            @pl.when(jnp.logical_not(here))
            def _():
                remote(b_own.at[it], b_left.at[it, slot_left], bl_ss.at[it, j], bl_rs.at[it, slot_left], owner_row, j).wait_send()

            g = row * C + j
            own_row, own_col = lax.rem(g, R), g // R
            there = jnp.logical_and(own_row == row, own_col == col)

            @pl.when(jnp.logical_not(there))
            def _():
                remote(c_rsend.at[it, j], c_rrecv.at[it, col], cr_ss.at[it, j], cr_rs.at[it, col], own_row, own_col).wait_send()

        @pl.loop(0, stack)
        def _(b):
            e_copy(b).wait_send()
            for k in range(1, Y):
                y_copy(b, k, ypos).wait_send()
            g_copy(b, core).wait_send()

    @pl.loop(1, R)
    def _(k):
        peer = away(k)
        remote(t_all.at[0, row], t_all.at[0, row], t_ss.at[0, peer], t_rs.at[0, row], peer, col).wait_send()

    @pl.loop(0, L)
    def _(z):
        block = z * 2 + side
        blk(block, p_x, pair).wait_send()

        @pl.when(jnp.logical_and(z <= line, line + 1 < L))
        def _():
            blk(block, p_up, row + 2).wait_send()

        @pl.when(jnp.logical_and(z >= line, line >= 1))
        def _():
            blk(block, p_dn, row - 2).wait_send()


def fused(mesh, start_vec, cond_orb, val_orb, kernel, cond_energy, val_energy):
    R, C = mesh.shape["row"], mesh.shape["col"]
    count, nc, nv = start_vec.shape
    stack = 2 * count
    half = nc // 2
    span_row, span_col = kernel.shape
    vs = val_orb.shape[0]
    chunk = span_row // C
    Y = C // 2
    f32, bf16 = jnp.float32, jnp.bfloat16
    V = pltpu.VMEM
    D = pltpu.SemaphoreType.DMA
    energy = cond_energy[:, None] - val_energy[None, :]
    vm = pl.BlockSpec(memory_space=pltpu.VMEM)
    scratch = [
        V((R, vs, span_col), bf16),
        V((span_row, span_col), bf16),
        V((2, ROWS_K, span_col), f32),
        V((ITERS, stack, nc, nv), f32),
        V((stack, nc, nv), bf16),
        V((stack, nc, nv), f32),
        V((nc, span_col), bf16),
        V((stack, span_col), bf16),
        V((stack, span_row), bf16),
        V((count, TERMS, 128), f32),
        V((R, count, chunk), f32),
        V((R, count, chunk), f32),
        V((R, stack, chunk), f32),
        V((R, stack, chunk), f32),
        V((ITERS, R, count, chunk), f32),
        V((ITERS, count, chunk), f32),
        V((ITERS, C, count, chunk), f32),
        V((ITERS, C, count, chunk), f32),
        V((ITERS, C, count, chunk), f32),
        V((ITERS, R, count, chunk), f32),
        V((ITERS, R, count, chunk), f32),
        V((ITERS, R, stack, chunk), f32),
        V((ITERS, stack, half, nv), f32),
        V((ITERS, stack, half, nv), f32),
        V((ITERS, Y, stack, half, nv), bf16),
        V((ITERS, 2, stack, half, nv), f32),
        V((ITERS + 1, R, 8, 128), f32),
        D((2,)),
        D((R,)), D((R,)), D((R,)), D((R,)),
        D((ITERS, R)), D((ITERS, R)),
        D((ITERS, R)), D((ITERS, R)),
        D((ITERS, C)), D((ITERS, C)),
        D((ITERS, C)), D((ITERS, C)),
        D((ITERS, R)), D((ITERS, R)),
        D((ITERS, R)), D((ITERS, R)),
        D((ITERS, stack)), D((ITERS, stack)),
        D((ITERS, Y, stack)), D((ITERS, Y, stack)),
        D((ITERS, stack)), D((ITERS, 2, stack)),
        D((ITERS + 1, R)), D((ITERS + 1, R)),
    ]
    right, left, coefs = pl.pallas_call(
        functools.partial(body_kernel, R, C),
        out_shape=(
            jax.ShapeDtypeStruct((count, nc, nv), f32),
            jax.ShapeDtypeStruct((count, nc, nv), f32),
            jax.ShapeDtypeStruct((2 * ITERS, 128), f32),
        ),
        in_specs=[vm, vm, vm, pl.BlockSpec(memory_space=pl.ANY), vm],
        out_specs=(vm, vm, vm),
        scratch_shapes=scratch,
        compiler_params=pltpu.CompilerParams(
            collective_id=0, has_side_effects=True, vmem_limit_bytes=62 * 2**20
        ),
    )(start_vec, cond_orb, val_orb, kernel, energy)
    coefs = coefs[:, :count].T
    beta = coefs[:, -1][:, None, None]
    return right / beta, left / beta, coefs


def solution(mesh):
    in_specs = (
        P(None, "row", None),
        P("row", "col"),
        P("row", "col"),
        P("row", "col"),
        P("row"),
        P(),
    )
    out_specs = (P(None, "row", None), P(None, "row", None), P())

    def run(*arrays):
        body = fused if fits(mesh, *arrays) else shards
        return jax.shard_map(
            functools.partial(body, mesh) if body is fused else body,
            mesh=mesh,
            in_specs=in_specs,
            out_specs=out_specs,
            check_vma=False,
        )(*arrays)

    return run
```

```python
import functools

import jax
import jax.numpy as jnp
from jax import lax
from jax.experimental import pallas as pl
from jax.experimental.pallas import tpu as pltpu
from jax.sharding import PartitionSpec as P

ITERS = 2


def inner_local(first, second):
    return jnp.sum(first * second, axis=(1, 2))


def shards(start_vec, cond_orb, val_orb, kernel, cond_energy, val_energy):
    count = start_vec.shape[0]
    row_place = lax.axis_index("row")
    col_place = lax.axis_index("col")
    span_row = kernel.shape[0]
    span_col = kernel.shape[1]
    panel = lax.all_gather(val_orb, "row", axis=0, tiled=True)
    cond_f = cond_orb.astype(jnp.float32)
    energy = cond_energy[:, None] - val_energy[None, :]

    def row_total(values):
        return lax.psum(values, "row")

    def col_total(values):
        return lax.psum(values, "col")

    def reduce_dots(terms):
        return row_total(terms)

    (norm_sq,) = reduce_dots((inner_local(start_vec, start_vec),))
    right = start_vec / jnp.sqrt(norm_sq)[:, None, None]
    left = right
    right_old = jnp.zeros_like(right)
    left_old = jnp.zeros_like(left)
    record = []
    for step in range(ITERS):
        stack = jnp.concatenate([right, left], axis=0)
        rounded = stack.astype(jnp.bfloat16)
        paired = jnp.einsum("bcv,vn->bcn", rounded, panel, preferred_element_type=jnp.float32)
        partial_value = jnp.sum(paired * cond_f[None], axis=1)
        folded = row_total(partial_value)
        right_coeff = folded[:count]
        left_coeff = folded[count:]
        left_all = lax.all_gather(left_coeff, "col", axis=1, tiled=True)
        left_rows = lax.dynamic_slice_in_dim(left_all, row_place * span_row, span_row, 1)
        right_part = jnp.einsum(
            "bn,mn->bm",
            right_coeff,
            kernel,
            precision=lax.Precision.HIGHEST,
            preferred_element_type=jnp.float32,
        )
        left_part = jnp.einsum(
            "bm,mn->bn",
            left_rows,
            kernel,
            precision=lax.Precision.HIGHEST,
            preferred_element_type=jnp.float32,
        )
        right_zed = col_total(right_part)
        left_zed = row_total(left_part)
        right_all = lax.all_gather(right_zed, "row", axis=1, tiled=True)
        right_cols = lax.dynamic_slice_in_dim(right_all, col_place * span_col, span_col, 1)
        zed = jnp.concatenate([right_cols, left_zed], axis=0)
        weighted = (cond_f[None] * zed[:, None, :]).astype(jnp.bfloat16)
        image_terms = jnp.einsum("bcn,vn->bcv", weighted, panel, preferred_element_type=jnp.float32)
        kernel_part = col_total(image_terms)
        images = energy[None] * stack + kernel_part
        image_r = images[:count]
        image_l = images[count:]
        table = reduce_dots(
            (
                inner_local(left, image_r),
                inner_local(left_old, image_r),
                inner_local(right_old, image_l),
                inner_local(image_l, image_r),
                inner_local(image_l, right),
                inner_local(left, right),
                inner_local(left, right_old),
                inner_local(left_old, right),
                inner_local(left_old, right_old),
                inner_local(image_r, image_r),
                inner_local(right, right),
                inner_local(right_old, right_old),
                inner_local(image_r, right),
                inner_local(image_r, right_old),
                inner_local(right, right_old),
                inner_local(image_l, image_l),
                inner_local(left, left),
                inner_local(left_old, left_old),
                inner_local(image_l, left),
                inner_local(image_l, left_old),
                inner_local(left, left_old),
            )
        )
        alpha, mu_co, nu_co = (table[0], table[1], table[2])
        cross = (
            table[3]
            - alpha * table[4]
            - mu_co * nu_co
            - alpha * alpha
            + alpha * alpha * table[5]
            + alpha * mu_co * table[6]
            - nu_co * mu_co
            + nu_co * alpha * table[7]
            + nu_co * mu_co * table[8]
        )
        right_sq = (
            table[9]
            + alpha * alpha * table[10]
            + mu_co * mu_co * table[11]
            - 2.0 * alpha * table[12]
            - 2.0 * mu_co * table[13]
            + 2.0 * alpha * mu_co * table[14]
        )
        left_sq = (
            table[15]
            + alpha * alpha * table[16]
            + nu_co * nu_co * table[17]
            - 2.0 * alpha * table[18]
            - 2.0 * nu_co * table[19]
            + 2.0 * alpha * nu_co * table[20]
        )
        resid_r = image_r - alpha[:, None, None] * right - mu_co[:, None, None] * right_old
        resid_l = image_l - alpha[:, None, None] * left - nu_co[:, None, None] * left_old
        bound = jnp.maximum(cross, 0.25 * jnp.sqrt(right_sq * left_sq))
        beta = jnp.sqrt(bound)
        right_old, left_old = (right, left)
        right = resid_r / beta[:, None, None]
        left = resid_l / beta[:, None, None]
        record.append(alpha)
        record.append(beta)
    joined = jnp.concatenate([right, left], axis=0)
    return (joined[:count], joined[count:], jnp.stack(record, axis=1))


MESH = pl.DeviceIdType.MESH
TERMS = 24
ROWS_K = 256


def fits(mesh, start_vec, cond_orb, val_orb, kernel, cond_energy, val_energy):
    R, C = mesh.shape["row"], mesh.shape["col"]
    points = kernel.shape[0]
    chunk = points // (R * C)
    local = cond_orb.shape[0] // R
    kernel_bytes = 2 * (points // R) * (points // C)
    return (
        start_vec.shape[0] == 4
        and R % 2 == 0
        and C == 4
        and chunk % ROWS_K == 0
        and local % 32 == 0
        and (val_orb.shape[0] // R) % 16 == 0
        and val_orb.shape[0] == 256
        and kernel_bytes <= 16 * 2**20
    )


def body_kernel(
    R, C,
    start, cond, val, kmat, energy,
    out_r, out_l, out_c,
    panel, kb, kf, xs, xb, img, wbuf, lhs_r, lhs_l, terms,
    a0_send, a0_recv, a1_send, a1_recv, b_row, b_own, b_left, c_rsend, c_rrecv, c_lsend, c_lrecv, d_r, d_l,
    e_send, e_recv, y_all, g_all, t_all,
    k_sem, p_up, p_dn, p_x, p_recv,
    a_ss, a_rs, b_ss, b_rs, bl_ss, bl_rs, cr_ss, cr_rs, cl_ss, cl_rs, dr_ss, dr_rs, dl_ss, dl_rs,
    e_ss, e_rs, y_ss, y_rs, g_ss, g_rs, t_ss, t_rs,
):
    row = lax.axis_index("row")
    col = lax.axis_index("col")
    count = start.shape[0]
    stack = 2 * count
    nc = start.shape[1]
    nv = start.shape[2]
    half = nc // 2
    chunk = a0_send.shape[-1]
    span_row = kb.shape[0]
    span_col = kb.shape[1]
    Y = C // 2
    core = lax.rem(col, 2)
    ypos = col // 2
    mate = ypos * 2 + 1 - core
    f32, bf16 = jnp.float32, jnp.bfloat16
    mine = col * R + row
    owner_row = mine // C
    slot_left = lax.rem(mine, C)

    def remote(src, dst, ss, rs, to_row, to_col):
        return pltpu.make_async_remote_copy(
            src_ref=src, dst_ref=dst, send_sem=ss, recv_sem=rs,
            device_id=(to_row, to_col), device_id_type=MESH,
        )

    def away(k):
        return lax.rem(row + k, R)

    barrier = pltpu.get_barrier_semaphore()

    @pl.loop(1, R * C)
    def _(k):
        flat = lax.rem(row * C + col + k, R * C)
        pl.semaphore_signal(barrier, inc=1, device_id=(flat // C, lax.rem(flat, C)), device_id_type=MESH)

    def kcopy(i, slot):
        return pltpu.make_async_copy(
            kmat.at[pl.ds(i * ROWS_K, ROWS_K), :], kf.at[slot], k_sem.at[slot]
        )

    kcopy(0, 0).start()
    kcopy(1, 1).start()
    panel[row] = val[...]

    for b in range(count):
        sq = jnp.sum(start[b] * start[b], axis=0, keepdims=True)
        terms[b, 0:1, :] = sq[:, :128] + sq[:, 128:]
    lane = lax.broadcasted_iota(jnp.int32, (8, 128), 1)
    tile = jnp.zeros((8, 128), f32)
    for b in range(count):
        total = jnp.sum(terms[b, 0:1, :], axis=1, keepdims=True)
        tile = tile + jnp.where(lane == b, total, 0.0)
    t_all[0, row] = tile

    pl.semaphore_wait(barrier, R * C - 1)

    def table_start(i):
        @pl.loop(1, R)
        def _(k):
            peer = away(k)
            remote(t_all.at[i, row], t_all.at[i, row], t_ss.at[i, peer], t_rs.at[i, row], peer, col).start()

    def table_wait(i):
        @pl.loop(1, R)
        def _(k):
            peer = away(k)
            remote(t_all.at[i, row], t_all.at[i, peer], t_ss.at[i, peer], t_rs.at[i, peer], peer, col).wait_recv()
        total = t_all[i, 0]
        for k in range(1, R):
            total = total + t_all[i, k]
        return total

    table_start(0)

    L = R // 2
    line = row // 2
    side = lax.rem(row, 2)
    pair = line * 2 + 1 - side

    def blk(block, sem, to_row):
        return remote(panel.at[block], panel.at[block], sem.at[block], p_recv.at[block], to_row, col)

    def pass_on(block, up, down):
        if up:
            @pl.when(line + 1 < L)
            def _():
                blk(block, p_up, row + 2).start()
        if down:
            @pl.when(line >= 1)
            def _():
                blk(block, p_dn, row - 2).start()
        blk(block, p_x, pair).start()

    pass_on(row, True, True)

    n_k = span_row // ROWS_K

    def take_k(i):
        slot = lax.rem(i, 2)
        kcopy(i, slot).wait()
        base = pl.multiple_of(i * ROWS_K, ROWS_K)

        @pl.loop(0, ROWS_K // 16)
        def _(g):
            at = pl.multiple_of(g * 16, 16)
            kb[pl.ds(pl.multiple_of(base + at, 16), 16), :] = kf[slot, pl.ds(at, 16), :].astype(bf16)

        @pl.when(i + 2 < n_k)
        def _():
            kcopy(i + 2, slot).start()

    per = n_k // L
    for d in range(L):
        @pl.loop(d * per, n_k if d == L - 1 else (d + 1) * per)
        def _(i):
            take_k(i)
        if d == 0:
            total = table_wait(0)
            scale = 1.0 / jnp.sqrt(total[0:1, :])
            for b in range(count):
                q = start[b] * scale[:, b:b + 1]
                xs[0, b] = q
                xs[0, count + b] = q
                xb[b] = q.astype(bf16)
        if d + 1 < L:
            @pl.when(line - (d + 1) >= 0)
            def _():
                block = row - 2 * (d + 1)
                blk(block, p_x, pair).wait_recv()
                pass_on(block, True, False)

            @pl.when(line + (d + 1) < L)
            def _():
                block = row + 2 * (d + 1)
                blk(block, p_x, pair).wait_recv()
                pass_on(block, False, True)

    @pl.loop(0, L)
    def _(z):
        blk(z * 2 + 1 - side, p_x, pair).wait_recv()

    for it in range(ITERS):
        wide = count if it == 0 else stack
        a_send, a_recv = (a0_send, a0_recv) if it == 0 else (a1_send, a1_recv)

        @pl.loop(1, R + 1)
        def _(k):
            peer = away(k)
            at = pl.multiple_of(peer * chunk, chunk)
            block = panel[:, :, pl.ds(at, chunk)].reshape(nv, chunk)
            weight = cond[:, pl.ds(at, chunk)].astype(f32)
            for b in range(wide):
                paired = jnp.dot(xb[b], block, preferred_element_type=f32)
                value = jnp.sum(paired * weight, axis=0, keepdims=True)
                a_send[peer, b:b + 1, :] = value

            @pl.when(k < R)
            def _():
                remote(a_send.at[peer], a_recv.at[row], a_ss.at[it, peer], a_rs.at[it, row], peer, col).start()

        @pl.loop(1, R)
        def _(k):
            peer = away(k)
            remote(a_send.at[peer], a_recv.at[peer], a_ss.at[it, peer], a_rs.at[it, peer], peer, col).wait_recv()
        a_recv[row] = a_send[row]
        coeff = a_recv[0]
        for k in range(1, R):
            coeff = coeff + a_recv[k]
        right_coeff = coeff[:count]
        left_coeff = coeff if it == 0 else coeff[count:]

        b_row[it, row] = right_coeff
        b_own[it] = left_coeff
        for j in range(C):
            here = jnp.logical_and(owner_row == row, col == j)

            @pl.when(here)
            def _():
                b_left[it, slot_left] = left_coeff

            @pl.when(jnp.logical_not(here))
            def _():
                remote(b_own.at[it], b_left.at[it, slot_left], bl_ss.at[it, j], bl_rs.at[it, slot_left], owner_row, j).start()

        @pl.loop(1, R)
        def _(k):
            peer = away(k)
            remote(b_row.at[it, row], b_row.at[it, row], b_ss.at[it, peer], b_rs.at[it, row], peer, col).start()

        def split(ref, dst, pieces):
            for j in range(pieces):
                piece = ref[it, j]
                high = piece.astype(bf16).astype(f32)
                dst[:, j * chunk:(j + 1) * chunk] = jnp.concatenate([high, piece - high], axis=0).astype(bf16)

        for s in range(C):
            g = row * C + s
            own_row, own_col = lax.rem(g, R), g // R
            here = jnp.logical_and(own_row == row, own_col == col)

            @pl.when(jnp.logical_not(here))
            def _():
                remote(b_own.at[it], b_left.at[it, s], bl_ss.at[it, s], bl_rs.at[it, s], own_row, own_col).wait_recv()
        split(b_left, lhs_l, C)

        @pl.loop(1, R + 1)
        def _(k):
            peer = away(k)
            at = pl.multiple_of(peer * chunk, chunk)
            left = jnp.dot(lhs_l[...], kb[:, pl.ds(at, chunk)], preferred_element_type=f32)
            c_lsend[it, peer] = left[:count] + left[count:]

            @pl.when(k < R)
            def _():
                remote(c_lsend.at[it, peer], c_lrecv.at[it, row], cl_ss.at[it, peer], cl_rs.at[it, row], peer, col).start()

        c_lrecv[it, row] = c_lsend[it, row]

        @pl.loop(1, R)
        def _(k):
            peer = away(k)
            remote(b_row.at[it, row], b_row.at[it, peer], b_ss.at[it, peer], b_rs.at[it, peer], peer, col).wait_recv()
        split(b_row, lhs_r, R)

        @pl.loop(0, C)
        def _(s):
            g = row * C + s
            own_row, own_col = lax.rem(g, R), g // R
            part = kb[pl.ds(pl.multiple_of(s * chunk, chunk), chunk), :]
            right = lax.dot_general(lhs_r[...], part, (((1,), (1,)), ((), ())), preferred_element_type=f32)
            c_rsend[it, s] = right[:count] + right[count:]
            here = jnp.logical_and(own_row == row, own_col == col)

            @pl.when(here)
            def _():
                c_rrecv[it, col] = c_rsend[it, s]

            @pl.when(jnp.logical_not(here))
            def _():
                remote(c_rsend.at[it, s], c_rrecv.at[it, col], cr_ss.at[it, s], cr_rs.at[it, col], own_row, own_col).start()

        @pl.loop(1, R)
        def _(k):
            peer = away(k)
            remote(c_lsend.at[it, peer], c_lrecv.at[it, peer], cl_ss.at[it, peer], cl_rs.at[it, peer], peer, col).wait_recv()
        zl = c_lrecv[it, 0]
        for j in range(1, R):
            zl = zl + c_lrecv[it, j]
        d_l[it, row] = zl

        @pl.loop(1, R)
        def _(k):
            peer = away(k)
            remote(d_l.at[it, row], d_l.at[it, row], dl_ss.at[it, peer], dl_rs.at[it, row], peer, col).start()

        for j in range(C):
            here = jnp.logical_and(owner_row == row, col == j)

            @pl.when(jnp.logical_not(here))
            def _():
                remote(c_rsend.at[it, j], c_rrecv.at[it, j], cr_ss.at[it, j], cr_rs.at[it, j], owner_row, j).wait_recv()

        zr = c_rrecv[it, 0]
        for j in range(1, C):
            zr = zr + c_rrecv[it, j]
        d_r[it, row] = zr

        @pl.loop(1, R)
        def _(k):
            peer = away(k)
            remote(d_r.at[it, row], d_r.at[it, row], dr_ss.at[it, peer], dr_rs.at[it, row], peer, col).start()

        @pl.loop(1, R)
        def _(k):
            peer = away(k)
            remote(d_l.at[it, row], d_l.at[it, peer], dl_ss.at[it, peer], dl_rs.at[it, peer], peer, col).wait_recv()

        def e_copy(b):
            return remote(e_send.at[it, b], e_recv.at[it, b], e_ss.at[it, b], e_rs.at[it, b], row, mate)

        def y_copy(b, k, sender):
            other = lax.rem(ypos + k, Y)
            return remote(
                y_all.at[it, ypos, b], y_all.at[it, sender, b], y_ss.at[it, k, b], y_rs.at[it, sender, b],
                row, other * 2 + core,
            )

        def g_copy(b, sender):
            return remote(g_all.at[it, core, b], g_all.at[it, sender, b], g_ss.at[it, b], g_rs.at[it, sender, b], row, mate)

        own = pl.ds(pl.multiple_of(core * half, half), half)
        rest = pl.ds(pl.multiple_of((1 - core) * half, half), half)

        def backward(b, zed, i):
            for j in range(R):
                at = slice(j * chunk, (j + 1) * chunk)
                z = zed[it, j, pl.ds(i, 1), :]
                wbuf[:, at] = (cond[:, at].astype(f32) * z).astype(bf16)
            total = jnp.zeros((nc, nv), f32)
            for j in range(R):
                at = slice(j * chunk, (j + 1) * chunk)
                total = total + lax.dot_general(
                    wbuf[:, at], panel[:, :, at].reshape(nv, chunk), (((1,), (1,)), ((), ())),
                    preferred_element_type=f32,
                )
            img[b] = total
            e_send[it, b] = img[b, rest, :]
            e_copy(b).start()

        def cross(b):
            e_copy(b).wait_recv()
            y_all[it, ypos, b] = (img[b, own, :] + e_recv[it, b]).astype(bf16)
            for k in range(1, Y):
                y_copy(b, k, ypos).start()

        def finish(b):
            for k in range(1, Y):
                y_copy(b, k, lax.rem(ypos + k, Y)).wait_recv()
            total = y_all[it, 0, b].astype(f32)
            for k in range(1, Y):
                total = total + y_all[it, k, b].astype(f32)
            g_all[it, core, b] = total
            g_copy(b, core).start()

        @pl.loop(0, count)
        def _(k):
            backward(count + k, d_l, k)

            @pl.when(k >= 1)
            def _():
                cross(count + k - 1)

        @pl.loop(1, R)
        def _(k):
            peer = away(k)
            remote(d_r.at[it, row], d_r.at[it, peer], dr_ss.at[it, peer], dr_rs.at[it, peer], peer, col).wait_recv()

        @pl.loop(0, count)
        def _(k):
            backward(k, d_r, k)
            cross(lax.rem(k + stack - 1, stack))
            finish(count + k)

        cross(count - 1)

        @pl.loop(0, count)
        def _(k):
            finish(k)

        @pl.loop(0, stack)
        def _(b):
            g_copy(b, 1 - core).wait_recv()
            for h in range(2):
                rows = slice(h * half, (h + 1) * half)
                img[b, rows, :] = energy[rows, :] * xs[it, b, rows, :] + g_all[it, h, b]

        for b in range(count):
            def add(g, acc):
                at = pl.ds(pl.multiple_of(g * 8, 8), 8)
                ir, il = img[b, at, :], img[count + b, at, :]
                q, p = xs[it, b, at, :], xs[it, count + b, at, :]
                if it == 0:
                    pairs = [(q, ir), (il, ir), (il, q), (q, q), (ir, ir), (il, il)]
                else:
                    qo, po = xs[it - 1, b, at, :], xs[it - 1, count + b, at, :]
                    pairs = [
                        (p, ir), (il, ir), (il, q), (p, q), (ir, ir), (q, q), (ir, q), (il, il), (p, p), (il, p),
                        (po, ir), (qo, il), (p, qo), (po, q), (po, qo), (qo, qo), (ir, qo), (q, qo), (po, po), (il, po), (p, po),
                    ]
                out = []
                for old, (u, w) in zip(acc, pairs):
                    prod = u * w
                    out.append(old + prod[:, :128] + prod[:, 128:])
                return tuple(out)
            n_terms = 6 if it == 0 else 21
            acc = lax.fori_loop(0, nc // 8, add, tuple(jnp.zeros((8, 128), f32) for _ in range(n_terms)))
            for t in range(n_terms):
                terms[b, t:t + 1, :] = jnp.sum(acc[t], axis=0, keepdims=True)
            terms[b, n_terms:TERMS, :] = jnp.zeros((TERMS - n_terms, 128), f32)
        tile = jnp.zeros((8, 128), f32)
        groups = 1 if it == 0 else TERMS // 8
        for b in range(count):
            sums = jnp.sum(terms[b], axis=1, keepdims=True)
            for g in range(groups):
                tile = tile + jnp.where(lane == count * g + b, sums[8 * g:8 * g + 8], 0.0)
        t_all[it + 1, row] = tile
        table_start(it + 1)
        table = table_wait(it + 1)
        packs = [table] + [pltpu.roll(table, 128 - count * g, 1) for g in range(1, groups)]
        T = [packs[t // 8][t % 8:t % 8 + 1, :] for t in range(8 * groups)]
        if it == 0:
            T = [T[0], T[1], T[2], T[3], T[4], T[3], T[0], T[5], T[3], T[2]]
        alpha = T[0]
        cross_term = T[1] - alpha * T[2] - alpha * alpha + alpha * alpha * T[3]
        right_sq = T[4] + alpha * alpha * T[5] - 2.0 * alpha * T[6]
        left_sq = T[7] + alpha * alpha * T[8] - 2.0 * alpha * T[9]
        if it:
            mu, nu = T[10], T[11]
            cross_term = (
                cross_term - mu * nu + alpha * mu * T[12] - nu * mu + nu * alpha * T[13] + nu * mu * T[14]
            )
            right_sq = right_sq + mu * mu * T[15] - 2.0 * mu * T[16] + 2.0 * alpha * mu * T[17]
            left_sq = left_sq + nu * nu * T[18] - 2.0 * nu * T[19] + 2.0 * alpha * nu * T[20]
        beta = jnp.sqrt(jnp.maximum(cross_term, 0.25 * jnp.sqrt(right_sq * left_sq)))
        out_c[2 * it:2 * it + 1, :] = alpha
        out_c[2 * it + 1:2 * it + 2, :] = beta
        inverse = 1.0 / beta
        for b in range(count):
            one = slice(b, b + 1)
            r = img[b] - alpha[:, one] * xs[it, b]
            s = img[count + b] - alpha[:, one] * xs[it, count + b]
            if it:
                r = r - mu[:, one] * xs[it - 1, b]
                s = s - nu[:, one] * xs[it - 1, count + b]
            if it + 1 == ITERS:
                out_r[b] = r
                out_l[b] = s
            else:
                r = r * inverse[:, one]
                s = s * inverse[:, one]
                xs[it + 1, b] = r
                xs[it + 1, count + b] = s
                xb[b] = r.astype(bf16)
                xb[count + b] = s.astype(bf16)

        @pl.loop(1, R)
        def _(k):
            peer = away(k)
            remote(a_send.at[peer], a_recv.at[row], a_ss.at[it, peer], a_rs.at[it, row], peer, col).wait_send()
            remote(b_row.at[it, row], b_row.at[it, row], b_ss.at[it, peer], b_rs.at[it, row], peer, col).wait_send()
            remote(c_lsend.at[it, peer], c_lrecv.at[it, row], cl_ss.at[it, peer], cl_rs.at[it, row], peer, col).wait_send()
            remote(d_r.at[it, row], d_r.at[it, row], dr_ss.at[it, peer], dr_rs.at[it, row], peer, col).wait_send()
            remote(d_l.at[it, row], d_l.at[it, row], dl_ss.at[it, peer], dl_rs.at[it, row], peer, col).wait_send()
            remote(t_all.at[it + 1, row], t_all.at[it + 1, row], t_ss.at[it + 1, peer], t_rs.at[it + 1, row], peer, col).wait_send()

        for j in range(C):
            here = jnp.logical_and(owner_row == row, col == j)

            @pl.when(jnp.logical_not(here))
            def _():
                remote(b_own.at[it], b_left.at[it, slot_left], bl_ss.at[it, j], bl_rs.at[it, slot_left], owner_row, j).wait_send()

            g = row * C + j
            own_row, own_col = lax.rem(g, R), g // R
            there = jnp.logical_and(own_row == row, own_col == col)

            @pl.when(jnp.logical_not(there))
            def _():
                remote(c_rsend.at[it, j], c_rrecv.at[it, col], cr_ss.at[it, j], cr_rs.at[it, col], own_row, own_col).wait_send()

        @pl.loop(0, stack)
        def _(b):
            e_copy(b).wait_send()
            for k in range(1, Y):
                y_copy(b, k, ypos).wait_send()
            g_copy(b, core).wait_send()

    @pl.loop(1, R)
    def _(k):
        peer = away(k)
        remote(t_all.at[0, row], t_all.at[0, row], t_ss.at[0, peer], t_rs.at[0, row], peer, col).wait_send()

    @pl.loop(0, L)
    def _(z):
        block = z * 2 + side
        blk(block, p_x, pair).wait_send()

        @pl.when(jnp.logical_and(z <= line, line + 1 < L))
        def _():
            blk(block, p_up, row + 2).wait_send()

        @pl.when(jnp.logical_and(z >= line, line >= 1))
        def _():
            blk(block, p_dn, row - 2).wait_send()


def fused(mesh, start_vec, cond_orb, val_orb, kernel, cond_energy, val_energy):
    R, C = mesh.shape["row"], mesh.shape["col"]
    count, nc, nv = start_vec.shape
    stack = 2 * count
    half = nc // 2
    span_row, span_col = kernel.shape
    vs = val_orb.shape[0]
    chunk = span_row // C
    Y = C // 2
    f32, bf16 = jnp.float32, jnp.bfloat16
    V = pltpu.VMEM
    D = pltpu.SemaphoreType.DMA
    energy = cond_energy[:, None] - val_energy[None, :]
    vm = pl.BlockSpec(memory_space=pltpu.VMEM)
    scratch = [
        V((R, vs, span_col), bf16),
        V((span_row, span_col), bf16),
        V((2, ROWS_K, span_col), f32),
        V((ITERS, stack, nc, nv), f32),
        V((stack, nc, nv), bf16),
        V((stack, nc, nv), f32),
        V((nc, span_col), bf16),
        V((stack, span_col), bf16),
        V((stack, span_row), bf16),
        V((count, TERMS, 128), f32),
        V((R, count, chunk), f32),
        V((R, count, chunk), f32),
        V((R, stack, chunk), f32),
        V((R, stack, chunk), f32),
        V((ITERS, R, count, chunk), f32),
        V((ITERS, count, chunk), f32),
        V((ITERS, C, count, chunk), f32),
        V((ITERS, C, count, chunk), f32),
        V((ITERS, C, count, chunk), f32),
        V((ITERS, R, count, chunk), f32),
        V((ITERS, R, count, chunk), f32),
        V((ITERS, R, count, chunk), f32),
        V((ITERS, R, count, chunk), f32),
        V((ITERS, stack, half, nv), f32),
        V((ITERS, stack, half, nv), f32),
        V((ITERS, Y, stack, half, nv), bf16),
        V((ITERS, 2, stack, half, nv), f32),
        V((ITERS + 1, R, 8, 128), f32),
        D((2,)),
        D((R,)), D((R,)), D((R,)), D((R,)),
        D((ITERS, R)), D((ITERS, R)),
        D((ITERS, R)), D((ITERS, R)),
        D((ITERS, C)), D((ITERS, C)),
        D((ITERS, C)), D((ITERS, C)),
        D((ITERS, R)), D((ITERS, R)),
        D((ITERS, R)), D((ITERS, R)),
        D((ITERS, R)), D((ITERS, R)),
        D((ITERS, stack)), D((ITERS, stack)),
        D((ITERS, Y, stack)), D((ITERS, Y, stack)),
        D((ITERS, stack)), D((ITERS, 2, stack)),
        D((ITERS + 1, R)), D((ITERS + 1, R)),
    ]
    right, left, coefs = pl.pallas_call(
        functools.partial(body_kernel, R, C),
        out_shape=(
            jax.ShapeDtypeStruct((count, nc, nv), f32),
            jax.ShapeDtypeStruct((count, nc, nv), f32),
            jax.ShapeDtypeStruct((2 * ITERS, 128), f32),
        ),
        in_specs=[vm, vm, vm, pl.BlockSpec(memory_space=pl.ANY), vm],
        out_specs=(vm, vm, vm),
        scratch_shapes=scratch,
        compiler_params=pltpu.CompilerParams(
            collective_id=0, has_side_effects=True, vmem_limit_bytes=62 * 2**20
        ),
    )(start_vec, cond_orb, val_orb, kernel, energy)
    coefs = coefs[:, :count].T
    beta = coefs[:, -1][:, None, None]
    return right / beta, left / beta, coefs


def solution(mesh):
    in_specs = (
        P(None, "row", None),
        P("row", "col"),
        P("row", "col"),
        P("row", "col"),
        P("row"),
        P(),
    )
    out_specs = (P(None, "row", None), P(None, "row", None), P())

    def run(*arrays):
        body = fused if fits(mesh, *arrays) else shards
        return jax.shard_map(
            functools.partial(body, mesh) if body is fused else body,
            mesh=mesh,
            in_specs=in_specs,
            out_specs=out_specs,
            check_vma=False,
        )(*arrays)

    return run
```

```python
import functools

import jax
import jax.numpy as jnp
from jax import lax
from jax.experimental import pallas as pl
from jax.experimental.pallas import tpu as pltpu
from jax.sharding import PartitionSpec as P

ITERS = 2


def inner_local(first, second):
    return jnp.sum(first * second, axis=(1, 2))


def shards(start_vec, cond_orb, val_orb, kernel, cond_energy, val_energy):
    count = start_vec.shape[0]
    row_place = lax.axis_index("row")
    col_place = lax.axis_index("col")
    span_row = kernel.shape[0]
    span_col = kernel.shape[1]
    panel = lax.all_gather(val_orb, "row", axis=0, tiled=True)
    cond_f = cond_orb.astype(jnp.float32)
    energy = cond_energy[:, None] - val_energy[None, :]

    def row_total(values):
        return lax.psum(values, "row")

    def col_total(values):
        return lax.psum(values, "col")

    def reduce_dots(terms):
        return row_total(terms)

    (norm_sq,) = reduce_dots((inner_local(start_vec, start_vec),))
    right = start_vec / jnp.sqrt(norm_sq)[:, None, None]
    left = right
    right_old = jnp.zeros_like(right)
    left_old = jnp.zeros_like(left)
    record = []
    for step in range(ITERS):
        stack = jnp.concatenate([right, left], axis=0)
        rounded = stack.astype(jnp.bfloat16)
        paired = jnp.einsum("bcv,vn->bcn", rounded, panel, preferred_element_type=jnp.float32)
        partial_value = jnp.sum(paired * cond_f[None], axis=1)
        folded = row_total(partial_value)
        right_coeff = folded[:count]
        left_coeff = folded[count:]
        left_all = lax.all_gather(left_coeff, "col", axis=1, tiled=True)
        left_rows = lax.dynamic_slice_in_dim(left_all, row_place * span_row, span_row, 1)
        right_part = jnp.einsum(
            "bn,mn->bm",
            right_coeff,
            kernel,
            precision=lax.Precision.HIGHEST,
            preferred_element_type=jnp.float32,
        )
        left_part = jnp.einsum(
            "bm,mn->bn",
            left_rows,
            kernel,
            precision=lax.Precision.HIGHEST,
            preferred_element_type=jnp.float32,
        )
        right_zed = col_total(right_part)
        left_zed = row_total(left_part)
        right_all = lax.all_gather(right_zed, "row", axis=1, tiled=True)
        right_cols = lax.dynamic_slice_in_dim(right_all, col_place * span_col, span_col, 1)
        zed = jnp.concatenate([right_cols, left_zed], axis=0)
        weighted = (cond_f[None] * zed[:, None, :]).astype(jnp.bfloat16)
        image_terms = jnp.einsum("bcn,vn->bcv", weighted, panel, preferred_element_type=jnp.float32)
        kernel_part = col_total(image_terms)
        images = energy[None] * stack + kernel_part
        image_r = images[:count]
        image_l = images[count:]
        table = reduce_dots(
            (
                inner_local(left, image_r),
                inner_local(left_old, image_r),
                inner_local(right_old, image_l),
                inner_local(image_l, image_r),
                inner_local(image_l, right),
                inner_local(left, right),
                inner_local(left, right_old),
                inner_local(left_old, right),
                inner_local(left_old, right_old),
                inner_local(image_r, image_r),
                inner_local(right, right),
                inner_local(right_old, right_old),
                inner_local(image_r, right),
                inner_local(image_r, right_old),
                inner_local(right, right_old),
                inner_local(image_l, image_l),
                inner_local(left, left),
                inner_local(left_old, left_old),
                inner_local(image_l, left),
                inner_local(image_l, left_old),
                inner_local(left, left_old),
            )
        )
        alpha, mu_co, nu_co = (table[0], table[1], table[2])
        cross = (
            table[3]
            - alpha * table[4]
            - mu_co * nu_co
            - alpha * alpha
            + alpha * alpha * table[5]
            + alpha * mu_co * table[6]
            - nu_co * mu_co
            + nu_co * alpha * table[7]
            + nu_co * mu_co * table[8]
        )
        right_sq = (
            table[9]
            + alpha * alpha * table[10]
            + mu_co * mu_co * table[11]
            - 2.0 * alpha * table[12]
            - 2.0 * mu_co * table[13]
            + 2.0 * alpha * mu_co * table[14]
        )
        left_sq = (
            table[15]
            + alpha * alpha * table[16]
            + nu_co * nu_co * table[17]
            - 2.0 * alpha * table[18]
            - 2.0 * nu_co * table[19]
            + 2.0 * alpha * nu_co * table[20]
        )
        resid_r = image_r - alpha[:, None, None] * right - mu_co[:, None, None] * right_old
        resid_l = image_l - alpha[:, None, None] * left - nu_co[:, None, None] * left_old
        bound = jnp.maximum(cross, 0.25 * jnp.sqrt(right_sq * left_sq))
        beta = jnp.sqrt(bound)
        right_old, left_old = (right, left)
        right = resid_r / beta[:, None, None]
        left = resid_l / beta[:, None, None]
        record.append(alpha)
        record.append(beta)
    joined = jnp.concatenate([right, left], axis=0)
    return (joined[:count], joined[count:], jnp.stack(record, axis=1))


MESH = pl.DeviceIdType.MESH
TERMS = 24
ROWS_K = 256


def fits(mesh, start_vec, cond_orb, val_orb, kernel, cond_energy, val_energy):
    R, C = mesh.shape["row"], mesh.shape["col"]
    points = kernel.shape[0]
    chunk = points // (R * C)
    local = cond_orb.shape[0] // R
    kernel_bytes = 2 * (points // R) * (points // C)
    return (
        start_vec.shape[0] == 4
        and R % 2 == 0
        and C == 4
        and chunk % ROWS_K == 0
        and local % 32 == 0
        and (val_orb.shape[0] // R) % 16 == 0
        and val_orb.shape[0] == 256
        and kernel_bytes <= 16 * 2**20
    )


def body_kernel(
    R, C,
    start, cond, val, kmat, energy,
    out_r, out_l, out_c,
    panel, kb, kf, xs, xb, img, wbuf, lhs_r, lhs_l, terms,
    a0_send, a0_recv, a1_send, a1_recv, b_row, b_own, b_left, c_rsend, c_rrecv, c_lsend, c_lrecv, d_r, d_l,
    e_send, e_recv, y_all, g_all, t_all,
    k_sem, p_up, p_dn, p_x, p_recv,
    a_ss, a_rs, b_ss, b_rs, bl_ss, bl_rs, cr_ss, cr_rs, cl_ss, cl_rs, dr_ss, dr_rs, dl_ss, dl_rs,
    e_ss, e_rs, y_ss, y_rs, g_ss, g_rs, t_ss, t_rs,
):
    row = lax.axis_index("row")
    col = lax.axis_index("col")
    count = start.shape[0]
    stack = 2 * count
    nc = start.shape[1]
    nv = start.shape[2]
    half = nc // 2
    chunk = a0_send.shape[-1]
    span_row = kb.shape[0]
    span_col = kb.shape[1]
    Y = C // 2
    core = lax.rem(col, 2)
    ypos = col // 2
    mate = ypos * 2 + 1 - core
    f32, bf16 = jnp.float32, jnp.bfloat16
    mine = col * R + row
    owner_row = mine // C
    slot_left = lax.rem(mine, C)

    def remote(src, dst, ss, rs, to_row, to_col):
        return pltpu.make_async_remote_copy(
            src_ref=src, dst_ref=dst, send_sem=ss, recv_sem=rs,
            device_id=(to_row, to_col), device_id_type=MESH,
        )

    def away(k):
        return lax.rem(row + k, R)

    barrier = pltpu.get_barrier_semaphore()

    @pl.loop(1, R * C)
    def _(k):
        flat = lax.rem(row * C + col + k, R * C)
        pl.semaphore_signal(barrier, inc=1, device_id=(flat // C, lax.rem(flat, C)), device_id_type=MESH)

    def kcopy(i, slot):
        return pltpu.make_async_copy(
            kmat.at[pl.ds(i * ROWS_K, ROWS_K), :], kf.at[slot], k_sem.at[slot]
        )

    kcopy(0, 0).start()
    kcopy(1, 1).start()
    panel[row] = val[...]

    for b in range(count):
        sq = jnp.sum(start[b] * start[b], axis=0, keepdims=True)
        terms[b, 0:1, :] = sq[:, :128] + sq[:, 128:]
    lane = lax.broadcasted_iota(jnp.int32, (8, 128), 1)
    tile = jnp.zeros((8, 128), f32)
    for b in range(count):
        total = jnp.sum(terms[b, 0:1, :], axis=1, keepdims=True)
        tile = tile + jnp.where(lane == b, total, 0.0)
    t_all[0, row] = tile

    pl.semaphore_wait(barrier, R * C - 1)

    def table_start(i):
        @pl.loop(1, R)
        def _(k):
            peer = away(k)
            remote(t_all.at[i, row], t_all.at[i, row], t_ss.at[i, peer], t_rs.at[i, row], peer, col).start()

    def table_wait(i):
        @pl.loop(1, R)
        def _(k):
            peer = away(k)
            remote(t_all.at[i, row], t_all.at[i, peer], t_ss.at[i, peer], t_rs.at[i, peer], peer, col).wait_recv()
        total = t_all[i, 0]
        for k in range(1, R):
            total = total + t_all[i, k]
        return total

    table_start(0)

    L = R // 2
    line = row // 2
    side = lax.rem(row, 2)
    pair = line * 2 + 1 - side

    def blk(block, sem, to_row):
        return remote(panel.at[block], panel.at[block], sem.at[block], p_recv.at[block], to_row, col)

    def pass_on(block, up, down):
        if up:
            @pl.when(line + 1 < L)
            def _():
                blk(block, p_up, row + 2).start()
        if down:
            @pl.when(line >= 1)
            def _():
                blk(block, p_dn, row - 2).start()
        blk(block, p_x, pair).start()

    pass_on(row, True, True)

    n_k = span_row // ROWS_K

    def take_k(i):
        slot = lax.rem(i, 2)
        kcopy(i, slot).wait()
        base = pl.multiple_of(i * ROWS_K, ROWS_K)

        @pl.loop(0, ROWS_K // 16)
        def _(g):
            at = pl.multiple_of(g * 16, 16)
            kb[pl.ds(pl.multiple_of(base + at, 16), 16), :] = kf[slot, pl.ds(at, 16), :].astype(bf16)

        @pl.when(i + 2 < n_k)
        def _():
            kcopy(i + 2, slot).start()

    per = n_k // L
    for d in range(L):
        @pl.loop(d * per, n_k if d == L - 1 else (d + 1) * per)
        def _(i):
            take_k(i)
        if d == 0:
            total = table_wait(0)
            scale = 1.0 / jnp.sqrt(total[0:1, :])
            for b in range(count):
                q = start[b] * scale[:, b:b + 1]
                xs[0, b] = q
                xs[0, count + b] = q
                xb[b] = q.astype(bf16)
        if d + 1 < L:
            @pl.when(line - (d + 1) >= 0)
            def _():
                block = row - 2 * (d + 1)
                blk(block, p_x, pair).wait_recv()
                pass_on(block, True, False)

            @pl.when(line + (d + 1) < L)
            def _():
                block = row + 2 * (d + 1)
                blk(block, p_x, pair).wait_recv()
                pass_on(block, False, True)

    @pl.loop(0, L)
    def _(z):
        blk(z * 2 + 1 - side, p_x, pair).wait_recv()

    for it in range(ITERS):
        wide = count if it == 0 else stack
        a_send, a_recv = (a0_send, a0_recv) if it == 0 else (a1_send, a1_recv)

        @pl.loop(1, R + 1)
        def _(k):
            peer = away(k)
            at = pl.multiple_of(peer * chunk, chunk)
            block = panel[:, :, pl.ds(at, chunk)].reshape(nv, chunk)
            weight = cond[:, pl.ds(at, chunk)].astype(f32)
            for b in range(wide):
                paired = jnp.dot(xb[b], block, preferred_element_type=f32)
                value = jnp.sum(paired * weight, axis=0, keepdims=True)
                a_send[peer, b:b + 1, :] = value

            @pl.when(k < R)
            def _():
                remote(a_send.at[peer], a_recv.at[row], a_ss.at[it, peer], a_rs.at[it, row], peer, col).start()

        @pl.loop(1, R)
        def _(k):
            peer = away(k)
            remote(a_send.at[peer], a_recv.at[peer], a_ss.at[it, peer], a_rs.at[it, peer], peer, col).wait_recv()
        a_recv[row] = a_send[row]
        coeff = a_recv[0]
        for k in range(1, R):
            coeff = coeff + a_recv[k]
        right_coeff = coeff[:count]
        left_coeff = coeff if it == 0 else coeff[count:]

        b_row[it, row] = right_coeff
        b_own[it] = left_coeff
        for j in range(C):
            here = jnp.logical_and(owner_row == row, col == j)

            @pl.when(here)
            def _():
                b_left[it, slot_left] = left_coeff

            @pl.when(jnp.logical_not(here))
            def _():
                remote(b_own.at[it], b_left.at[it, slot_left], bl_ss.at[it, j], bl_rs.at[it, slot_left], owner_row, j).start()

        @pl.loop(1, R)
        def _(k):
            peer = away(k)
            remote(b_row.at[it, row], b_row.at[it, row], b_ss.at[it, peer], b_rs.at[it, row], peer, col).start()

        def split(ref, dst, pieces):
            for j in range(pieces):
                piece = ref[it, j]
                high = piece.astype(bf16).astype(f32)
                dst[:, j * chunk:(j + 1) * chunk] = jnp.concatenate([high, piece - high], axis=0).astype(bf16)

        for s in range(C):
            g = row * C + s
            own_row, own_col = lax.rem(g, R), g // R
            here = jnp.logical_and(own_row == row, own_col == col)

            @pl.when(jnp.logical_not(here))
            def _():
                remote(b_own.at[it], b_left.at[it, s], bl_ss.at[it, s], bl_rs.at[it, s], own_row, own_col).wait_recv()
        split(b_left, lhs_l, C)

        @pl.loop(1, R + 1)
        def _(k):
            peer = away(k)
            at = pl.multiple_of(peer * chunk, chunk)
            left = jnp.dot(lhs_l[...], kb[:, pl.ds(at, chunk)], preferred_element_type=f32)
            c_lsend[it, peer] = left[:count] + left[count:]

            @pl.when(k < R)
            def _():
                remote(c_lsend.at[it, peer], c_lrecv.at[it, row], cl_ss.at[it, peer], cl_rs.at[it, row], peer, col).start()

        c_lrecv[it, row] = c_lsend[it, row]

        @pl.loop(1, R)
        def _(k):
            peer = away(k)
            remote(b_row.at[it, row], b_row.at[it, peer], b_ss.at[it, peer], b_rs.at[it, peer], peer, col).wait_recv()
        split(b_row, lhs_r, R)

        @pl.loop(0, C)
        def _(s):
            g = row * C + s
            own_row, own_col = lax.rem(g, R), g // R
            part = kb[pl.ds(pl.multiple_of(s * chunk, chunk), chunk), :]
            right = lax.dot_general(lhs_r[...], part, (((1,), (1,)), ((), ())), preferred_element_type=f32)
            c_rsend[it, s] = right[:count] + right[count:]
            here = jnp.logical_and(own_row == row, own_col == col)

            @pl.when(here)
            def _():
                c_rrecv[it, col] = c_rsend[it, s]

            @pl.when(jnp.logical_not(here))
            def _():
                remote(c_rsend.at[it, s], c_rrecv.at[it, col], cr_ss.at[it, s], cr_rs.at[it, col], own_row, own_col).start()

        @pl.loop(1, R)
        def _(k):
            peer = away(k)
            remote(c_lsend.at[it, peer], c_lrecv.at[it, peer], cl_ss.at[it, peer], cl_rs.at[it, peer], peer, col).wait_recv()
        zl = c_lrecv[it, 0]
        for j in range(1, R):
            zl = zl + c_lrecv[it, j]
        d_l[it, row] = zl

        @pl.loop(1, R)
        def _(k):
            peer = away(k)
            remote(d_l.at[it, row], d_l.at[it, row], dl_ss.at[it, peer], dl_rs.at[it, row], peer, col).start()

        for j in range(C):
            here = jnp.logical_and(owner_row == row, col == j)

            @pl.when(jnp.logical_not(here))
            def _():
                remote(c_rsend.at[it, j], c_rrecv.at[it, j], cr_ss.at[it, j], cr_rs.at[it, j], owner_row, j).wait_recv()

        zr = c_rrecv[it, 0]
        for j in range(1, C):
            zr = zr + c_rrecv[it, j]
        d_r[it, row] = zr

        @pl.loop(1, R)
        def _(k):
            peer = away(k)
            remote(d_r.at[it, row], d_r.at[it, row], dr_ss.at[it, peer], dr_rs.at[it, row], peer, col).start()

        @pl.loop(1, R)
        def _(k):
            peer = away(k)
            remote(d_l.at[it, row], d_l.at[it, peer], dl_ss.at[it, peer], dl_rs.at[it, peer], peer, col).wait_recv()

        def e_copy(b):
            return remote(e_send.at[it, b], e_recv.at[it, b], e_ss.at[it, b], e_rs.at[it, b], row, mate)

        def y_copy(b, k, sender):
            other = lax.rem(ypos + k, Y)
            return remote(
                y_all.at[it, ypos, b], y_all.at[it, sender, b], y_ss.at[it, k, b], y_rs.at[it, sender, b],
                row, other * 2 + core,
            )

        def g_copy(b, sender):
            return remote(g_all.at[it, core, b], g_all.at[it, sender, b], g_ss.at[it, b], g_rs.at[it, sender, b], row, mate)

        own = pl.ds(pl.multiple_of(core * half, half), half)
        rest = pl.ds(pl.multiple_of((1 - core) * half, half), half)

        def backward(b, zed, i):
            for j in range(R):
                at = slice(j * chunk, (j + 1) * chunk)
                z = zed[it, j, pl.ds(i, 1), :]
                wbuf[:, at] = (cond[:, at].astype(f32) * z).astype(bf16)
            total = lax.dot_general(
                wbuf[...], panel[...].reshape(nv, R * chunk), (((1,), (1,)), ((), ())),
                preferred_element_type=f32,
            )
            img[b] = total
            e_send[it, b] = img[b, rest, :]
            e_copy(b).start()

        def cross(b):
            e_copy(b).wait_recv()
            y_all[it, ypos, b] = (img[b, own, :] + e_recv[it, b]).astype(bf16)
            for k in range(1, Y):
                y_copy(b, k, ypos).start()

        def finish(b):
            for k in range(1, Y):
                y_copy(b, k, lax.rem(ypos + k, Y)).wait_recv()
            total = y_all[it, 0, b].astype(f32)
            for k in range(1, Y):
                total = total + y_all[it, k, b].astype(f32)
            g_all[it, core, b] = total
            g_copy(b, core).start()

        @pl.loop(0, count)
        def _(k):
            backward(count + k, d_l, k)

            @pl.when(k >= 1)
            def _():
                cross(count + k - 1)

        @pl.loop(1, R)
        def _(k):
            peer = away(k)
            remote(d_r.at[it, row], d_r.at[it, peer], dr_ss.at[it, peer], dr_rs.at[it, peer], peer, col).wait_recv()

        @pl.loop(0, count)
        def _(k):
            backward(k, d_r, k)
            cross(lax.rem(k + stack - 1, stack))
            finish(count + k)

        cross(count - 1)

        @pl.loop(0, count)
        def _(k):
            finish(k)

        @pl.loop(0, stack)
        def _(b):
            g_copy(b, 1 - core).wait_recv()
            for h in range(2):
                rows = slice(h * half, (h + 1) * half)
                img[b, rows, :] = energy[rows, :] * xs[it, b, rows, :] + g_all[it, h, b]

        for b in range(count):
            def add(g, acc):
                at = pl.ds(pl.multiple_of(g * 8, 8), 8)
                ir, il = img[b, at, :], img[count + b, at, :]
                q, p = xs[it, b, at, :], xs[it, count + b, at, :]
                if it == 0:
                    pairs = [(q, ir), (il, ir), (il, q), (q, q), (ir, ir), (il, il)]
                else:
                    qo, po = xs[it - 1, b, at, :], xs[it - 1, count + b, at, :]
                    pairs = [
                        (p, ir), (il, ir), (il, q), (p, q), (ir, ir), (q, q), (ir, q), (il, il), (p, p), (il, p),
                        (po, ir), (qo, il), (p, qo), (po, q), (po, qo), (qo, qo), (ir, qo), (q, qo), (po, po), (il, po), (p, po),
                    ]
                out = []
                for old, (u, w) in zip(acc, pairs):
                    prod = u * w
                    out.append(old + prod[:, :128] + prod[:, 128:])
                return tuple(out)
            n_terms = 6 if it == 0 else 21
            acc = lax.fori_loop(0, nc // 8, add, tuple(jnp.zeros((8, 128), f32) for _ in range(n_terms)))
            for t in range(n_terms):
                terms[b, t:t + 1, :] = jnp.sum(acc[t], axis=0, keepdims=True)
            terms[b, n_terms:TERMS, :] = jnp.zeros((TERMS - n_terms, 128), f32)
        tile = jnp.zeros((8, 128), f32)
        groups = 1 if it == 0 else TERMS // 8
        for b in range(count):
            sums = jnp.sum(terms[b], axis=1, keepdims=True)
            for g in range(groups):
                tile = tile + jnp.where(lane == count * g + b, sums[8 * g:8 * g + 8], 0.0)
        t_all[it + 1, row] = tile
        table_start(it + 1)
        table = table_wait(it + 1)
        packs = [table] + [pltpu.roll(table, 128 - count * g, 1) for g in range(1, groups)]
        T = [packs[t // 8][t % 8:t % 8 + 1, :] for t in range(8 * groups)]
        if it == 0:
            T = [T[0], T[1], T[2], T[3], T[4], T[3], T[0], T[5], T[3], T[2]]
        alpha = T[0]
        cross_term = T[1] - alpha * T[2] - alpha * alpha + alpha * alpha * T[3]
        right_sq = T[4] + alpha * alpha * T[5] - 2.0 * alpha * T[6]
        left_sq = T[7] + alpha * alpha * T[8] - 2.0 * alpha * T[9]
        if it:
            mu, nu = T[10], T[11]
            cross_term = (
                cross_term - mu * nu + alpha * mu * T[12] - nu * mu + nu * alpha * T[13] + nu * mu * T[14]
            )
            right_sq = right_sq + mu * mu * T[15] - 2.0 * mu * T[16] + 2.0 * alpha * mu * T[17]
            left_sq = left_sq + nu * nu * T[18] - 2.0 * nu * T[19] + 2.0 * alpha * nu * T[20]
        beta = jnp.sqrt(jnp.maximum(cross_term, 0.25 * jnp.sqrt(right_sq * left_sq)))
        out_c[2 * it:2 * it + 1, :] = alpha
        out_c[2 * it + 1:2 * it + 2, :] = beta
        inverse = 1.0 / beta
        for b in range(count):
            one = slice(b, b + 1)
            r = img[b] - alpha[:, one] * xs[it, b]
            s = img[count + b] - alpha[:, one] * xs[it, count + b]
            if it:
                r = r - mu[:, one] * xs[it - 1, b]
                s = s - nu[:, one] * xs[it - 1, count + b]
            if it + 1 == ITERS:
                out_r[b] = r
                out_l[b] = s
            else:
                r = r * inverse[:, one]
                s = s * inverse[:, one]
                xs[it + 1, b] = r
                xs[it + 1, count + b] = s
                xb[b] = r.astype(bf16)
                xb[count + b] = s.astype(bf16)

        @pl.loop(1, R)
        def _(k):
            peer = away(k)
            remote(a_send.at[peer], a_recv.at[row], a_ss.at[it, peer], a_rs.at[it, row], peer, col).wait_send()
            remote(b_row.at[it, row], b_row.at[it, row], b_ss.at[it, peer], b_rs.at[it, row], peer, col).wait_send()
            remote(c_lsend.at[it, peer], c_lrecv.at[it, row], cl_ss.at[it, peer], cl_rs.at[it, row], peer, col).wait_send()
            remote(d_r.at[it, row], d_r.at[it, row], dr_ss.at[it, peer], dr_rs.at[it, row], peer, col).wait_send()
            remote(d_l.at[it, row], d_l.at[it, row], dl_ss.at[it, peer], dl_rs.at[it, row], peer, col).wait_send()
            remote(t_all.at[it + 1, row], t_all.at[it + 1, row], t_ss.at[it + 1, peer], t_rs.at[it + 1, row], peer, col).wait_send()

        for j in range(C):
            here = jnp.logical_and(owner_row == row, col == j)

            @pl.when(jnp.logical_not(here))
            def _():
                remote(b_own.at[it], b_left.at[it, slot_left], bl_ss.at[it, j], bl_rs.at[it, slot_left], owner_row, j).wait_send()

            g = row * C + j
            own_row, own_col = lax.rem(g, R), g // R
            there = jnp.logical_and(own_row == row, own_col == col)

            @pl.when(jnp.logical_not(there))
            def _():
                remote(c_rsend.at[it, j], c_rrecv.at[it, col], cr_ss.at[it, j], cr_rs.at[it, col], own_row, own_col).wait_send()

        @pl.loop(0, stack)
        def _(b):
            e_copy(b).wait_send()
            for k in range(1, Y):
                y_copy(b, k, ypos).wait_send()
            g_copy(b, core).wait_send()

    @pl.loop(1, R)
    def _(k):
        peer = away(k)
        remote(t_all.at[0, row], t_all.at[0, row], t_ss.at[0, peer], t_rs.at[0, row], peer, col).wait_send()

    @pl.loop(0, L)
    def _(z):
        block = z * 2 + side
        blk(block, p_x, pair).wait_send()

        @pl.when(jnp.logical_and(z <= line, line + 1 < L))
        def _():
            blk(block, p_up, row + 2).wait_send()

        @pl.when(jnp.logical_and(z >= line, line >= 1))
        def _():
            blk(block, p_dn, row - 2).wait_send()


def fused(mesh, start_vec, cond_orb, val_orb, kernel, cond_energy, val_energy):
    R, C = mesh.shape["row"], mesh.shape["col"]
    count, nc, nv = start_vec.shape
    stack = 2 * count
    half = nc // 2
    span_row, span_col = kernel.shape
    vs = val_orb.shape[0]
    chunk = span_row // C
    Y = C // 2
    f32, bf16 = jnp.float32, jnp.bfloat16
    V = pltpu.VMEM
    D = pltpu.SemaphoreType.DMA
    energy = cond_energy[:, None] - val_energy[None, :]
    vm = pl.BlockSpec(memory_space=pltpu.VMEM)
    scratch = [
        V((R, vs, span_col), bf16),
        V((span_row, span_col), bf16),
        V((2, ROWS_K, span_col), f32),
        V((ITERS, stack, nc, nv), f32),
        V((stack, nc, nv), bf16),
        V((stack, nc, nv), f32),
        V((nc, span_col), bf16),
        V((stack, span_col), bf16),
        V((stack, span_row), bf16),
        V((count, TERMS, 128), f32),
        V((R, count, chunk), f32),
        V((R, count, chunk), f32),
        V((R, stack, chunk), f32),
        V((R, stack, chunk), f32),
        V((ITERS, R, count, chunk), f32),
        V((ITERS, count, chunk), f32),
        V((ITERS, C, count, chunk), f32),
        V((ITERS, C, count, chunk), f32),
        V((ITERS, C, count, chunk), f32),
        V((ITERS, R, count, chunk), f32),
        V((ITERS, R, count, chunk), f32),
        V((ITERS, R, count, chunk), f32),
        V((ITERS, R, count, chunk), f32),
        V((ITERS, stack, half, nv), f32),
        V((ITERS, stack, half, nv), f32),
        V((ITERS, Y, stack, half, nv), bf16),
        V((ITERS, 2, stack, half, nv), f32),
        V((ITERS + 1, R, 8, 128), f32),
        D((2,)),
        D((R,)), D((R,)), D((R,)), D((R,)),
        D((ITERS, R)), D((ITERS, R)),
        D((ITERS, R)), D((ITERS, R)),
        D((ITERS, C)), D((ITERS, C)),
        D((ITERS, C)), D((ITERS, C)),
        D((ITERS, R)), D((ITERS, R)),
        D((ITERS, R)), D((ITERS, R)),
        D((ITERS, R)), D((ITERS, R)),
        D((ITERS, stack)), D((ITERS, stack)),
        D((ITERS, Y, stack)), D((ITERS, Y, stack)),
        D((ITERS, stack)), D((ITERS, 2, stack)),
        D((ITERS + 1, R)), D((ITERS + 1, R)),
    ]
    right, left, coefs = pl.pallas_call(
        functools.partial(body_kernel, R, C),
        out_shape=(
            jax.ShapeDtypeStruct((count, nc, nv), f32),
            jax.ShapeDtypeStruct((count, nc, nv), f32),
            jax.ShapeDtypeStruct((2 * ITERS, 128), f32),
        ),
        in_specs=[vm, vm, vm, pl.BlockSpec(memory_space=pl.ANY), vm],
        out_specs=(vm, vm, vm),
        scratch_shapes=scratch,
        compiler_params=pltpu.CompilerParams(
            collective_id=0, has_side_effects=True, vmem_limit_bytes=62 * 2**20
        ),
    )(start_vec, cond_orb, val_orb, kernel, energy)
    coefs = coefs[:, :count].T
    beta = coefs[:, -1][:, None, None]
    return right / beta, left / beta, coefs


def solution(mesh):
    in_specs = (
        P(None, "row", None),
        P("row", "col"),
        P("row", "col"),
        P("row", "col"),
        P("row"),
        P(),
    )
    out_specs = (P(None, "row", None), P(None, "row", None), P())

    def run(*arrays):
        body = fused if fits(mesh, *arrays) else shards
        return jax.shard_map(
            functools.partial(body, mesh) if body is fused else body,
            mesh=mesh,
            in_specs=in_specs,
            out_specs=out_specs,
            check_vma=False,
        )(*arrays)

    return run
```
